256 devices in a mesh: feature: 4 (over x), kvhead: 8 (over y, core), seq: 8 (over z).
Axes of the slice: x: 4, y: 4, z: 8, core: 2. Of those that a mesh axis runs over, the one named last changes fastest.
Arguments:
- queries: float32 [2048, 40, 128], P('seq', 'kvhead'), may hold values from -6 to 6
- keys: float32 [2048, 8, 128], P('seq', 'kvhead'), may hold values from -6 to 6
- values: float32 [2048, 8, 128], P('seq', 'kvhead'), may hold values from -6 to 6
- w_out: float32 [5120, 5120], P('kvhead', ('feature', 'seq')), may hold values from -0.078125 to 0.078125
Outputs:
- projected: float32 [2048, 5120], P(('seq', 'feature'), 'kvhead')
The draws below stay inside these ranges and needn't reach their ends.
All inputs are finite; a program needn't handle non-finite values.
Results may differ from the reference program's by a relative error of at most 0.0003.
Values sent between devices are 32-bit elements; how exact they have to be, the bound alone decides.
A program may use at most 128 MiB of HBM per device.

```python
import jax
import jax.numpy as jnp
from jax import lax

D = 5120
QH = 40
KVH = 8
HD = 128
TOKENS = 2048


def block_levels(rng, shape, cuts, smallest, top_value):
    factor_of, own = 1.0, jax.random.fold_in(rng, 6)
    for dim, parts in cuts:
        heights = jnp.exp(jax.random.uniform(jax.random.fold_in(own, dim), (parts,), jnp.float32, smallest / len(cuts), top_value / len(cuts)))
        factor_of = factor_of * jnp.repeat(heights, shape[dim] // parts).reshape([-1 if axis == dim else 1 for axis in range(len(shape))])
    return factor_of


def gaussian(key, extent, deviation, limit, pieces=(), kind=jnp.bfloat16):
    entries = jax.random.normal(key, extent, jnp.float32) * deviation
    if len(pieces) > 0:
        entries = block_levels(key, extent, pieces, -0.22, 0.18) * entries
    return jnp.clip(entries, min=-limit, max=limit).astype(kind)


def setup_inputs(seed: int = 0) -> dict:
    streams_of = jax.random.split(jax.random.key(seed), 5)
    queries = gaussian(streams_of[0], (TOKENS, QH, HD), 1.0, 6.0, ((0, 8), (1, 8)), jnp.float32)
    keys = gaussian(streams_of[1], (TOKENS, KVH, HD), 1.0, 6.0, ((0, 8), (1, 8)), jnp.float32)
    values = gaussian(streams_of[2], (TOKENS, KVH, HD), 1.0, 6.0, ((0, 8), (1, 8)), jnp.float32)
    w_out = gaussian(streams_of[3], (QH * HD, D), (QH * HD) ** -0.5, 0.078125, ((0, 8), (1, 32)), jnp.float32)
    return dict(queries=queries, keys=keys, values=values, w_out=w_out)


def reference(queries, keys, values, w_out):
    block = 512 if TOKENS % 512 == 0 else TOKENS
    count = TOKENS // block
    group = QH // KVH
    scaled = (queries * (HD ** -0.5)).reshape(count, block, KVH, group, HD)
    key_blocks = keys.reshape(count, block, KVH, HD)
    value_blocks = values.reshape(count, block, KVH, HD)
    offsets = jnp.arange(block, dtype=jnp.int32)

    def one_block(index):
        query_part = lax.dynamic_index_in_dim(scaled, index, 0, keepdims=False)

        def key_step(other, carry):
            numerator, denominator = carry
            key_part = lax.dynamic_index_in_dim(key_blocks, other, 0, keepdims=False)
            value_part = lax.dynamic_index_in_dim(value_blocks, other, 0, keepdims=False)
            scores = jnp.einsum("tkgd,skd->tkgs", query_part, key_part, precision=lax.Precision.HIGHEST)
            squared = scores * scores
            query_pos = index * block + offsets
            key_pos = other * block + offsets
            allowed = key_pos[None, :] <= query_pos[:, None]
            squared = jnp.where(allowed[:, None, None, :], squared, jnp.float32(0.0))
            numerator = numerator + jnp.einsum("tkgs,skd->tkgd", squared, value_part, precision=lax.Precision.HIGHEST)
            denominator = denominator + jnp.sum(squared, axis=-1)
            return numerator, denominator

        start = (jnp.zeros((block, KVH, group, HD), jnp.float32), jnp.zeros((block, KVH, group), jnp.float32))
        numerator, denominator = lax.fori_loop(0, index + 1, key_step, start)
        attended = numerator / (denominator[..., None] + 1.0)
        return attended.reshape(block, QH * HD)

    attended = lax.map(one_block, jnp.arange(count, dtype=jnp.int32)).reshape(TOKENS, QH * HD)
    return jnp.dot(attended, w_out, precision=lax.Precision.HIGHEST, preferred_element_type=jnp.float32)
```

```python
import functools

import jax
import jax.numpy as jnp
from jax import lax
from jax.experimental import pallas as pl
from jax.experimental.pallas import tpu as pltpu
from jax.sharding import PartitionSpec as P

MESH = pl.DeviceIdType.MESH
NT = (((1,), (1,)), ((), ()))
F32 = jnp.float32
BF16 = jnp.bfloat16


def halves(x):
    high = x.astype(BF16)
    return high, (x - high.astype(F32)).astype(BF16)


def dot(a, b):
    return jnp.dot(a, b, preferred_element_type=F32)


def dot_nt(a, b):
    return lax.dot_general(a, b, NT, preferred_element_type=F32)


def kernel(
    q_hbm, k_hbm, v_hbm, w_hbm, o_ref,
    qv, kv, wt, qcat, kcat, klow, vcat, rs_src, rs_rcv, abuf, wh, wl, cpk, c1r, red, c2r,
    load_sem, kv_send, kv_recv, w_send, w_recv, rs_send, rs_recv, a_send, a_recv, c1_send, c1_recv, c2_send, c2_recv,
):
    group, rows, hd = q_hbm.shape
    parts = wt.shape[0]
    count = kv.shape[0]
    heads = c1r.shape[1]
    quarter = rows // parts
    half = count // 2
    wide = w_hbm.shape[0]
    rest = wide - hd
    lanes = hd // parts
    f = lax.axis_index("feature")
    k = lax.axis_index("kvhead")
    s = lax.axis_index("seq")
    y, c = lax.div(k, 2), lax.rem(k, 2)
    twin = k + 1 - 2 * c
    seq_half = lax.div(s, half)

    def at_z(d):
        return lax.rem(s + d + count, count)

    def at_x(d):
        return lax.rem(f + d + parts, parts)

    right, left = at_z(1), at_z(-1)

    own = pl.ds(pl.multiple_of(f * quarter, quarter), quarter)
    loads = [
        pltpu.make_async_copy(w_hbm, wt.at[f], load_sem.at[0]),
        pltpu.make_async_copy(k_hbm.at[own], kv.at[s, 0], load_sem.at[1]),
        pltpu.make_async_copy(v_hbm.at[own], kv.at[s, 1], load_sem.at[2]),
        pltpu.make_async_copy(q_hbm, qv, load_sem.at[3]),
    ]
    for load in loads:
        load.start()

    barrier = pltpu.get_barrier_semaphore()
    peers = 0
    for d in range(1, parts):
        pl.semaphore_signal(barrier, inc=1, device_id={"feature": at_x(d)}, device_id_type=MESH)
        peers += 1
    for d in range(1, count):
        pl.semaphore_signal(barrier, inc=1, device_id={"seq": at_z(d)}, device_id_type=MESH)
        pl.semaphore_signal(barrier, inc=1, device_id={"kvhead": twin, "seq": at_z(d)}, device_id_type=MESH)
        peers += 2
    for d in range(1, heads):
        pl.semaphore_signal(barrier, inc=1, device_id={"kvhead": lax.rem(k + d, heads)}, device_id_type=MESH)
        peers += 1
    for load in loads[:3]:
        load.wait()
    pl.semaphore_wait(barrier, peers)

    def remote(src, dst, send, recv, where):
        return pltpu.make_async_remote_copy(
            src_ref=src, dst_ref=dst, send_sem=send, recv_sem=recv, device_id=where, device_id_type=MESH
        )

    def kv_copy(i, slot, where):
        return remote(kv.at[slot], kv.at[slot], kv_send.at[i], kv_recv.at[i], {"seq": where})

    def kv_fwd(t):
        return kv_copy(t, at_z(-t), right)

    def kv_bwd(t):
        return kv_copy(half + t, at_z(t), left)

    def kv_take(slot):
        place = pl.ds(pl.multiple_of(slot * quarter, quarter), quarter)
        kh, kl = halves(kv[slot, 0])
        vh, vl = halves(kv[slot, 1])
        kcat[place, :hd] = kh
        kcat[place, hd:] = kh
        klow[place, :] = kl
        vcat[place, :hd] = vh
        vcat[place, hd:] = vl

    kv_fwd(0).start()
    kv_bwd(0).start()

    def w_copy(i, src, where):
        return remote(src, src, w_send.at[i], w_recv.at[i], {"feature": where})

    w_top, w_low = pl.ds(0, wide // 2), pl.ds(wide // 2, wide // 2)
    w_steps = [
        w_copy(0, wt.at[f], at_x(1)),
        w_copy(1, wt.at[f], at_x(-1)),
        w_copy(2, wt.at[at_x(-1), w_top], at_x(1)),
        w_copy(3, wt.at[at_x(1), w_low], at_x(-1)),
    ]
    w_takes = [
        w_copy(0, wt.at[at_x(-1)], at_x(1)),
        w_copy(1, wt.at[at_x(1)], at_x(-1)),
        w_copy(2, wt.at[at_x(2), w_top], at_x(1)),
        w_copy(3, wt.at[at_x(2), w_low], at_x(-1)),
    ]
    w_steps[0].start()
    w_steps[1].start()

    loads[3].wait()
    for g in range(group):
        qh, ql = halves(qv[g] * (hd ** -0.5))
        qcat[g, :, :hd] = qh
        qcat[g, :, hd:] = ql
    kv_take(s)
    for t in range(1, half + 1):
        kv_copy(t - 1, at_z(-t), right).wait_recv()
        if t < half:
            kv_fwd(t).start()
            kv_copy(half + t - 1, at_z(t), left).wait_recv()
            if t < half - 1:
                kv_bwd(t).start()
            kv_take(at_z(t))
        kv_take(at_z(-t))

    def rs_copy(d, g):
        to = at_x(d)
        return remote(rs_src.at[g, to], rs_rcv.at[d - 1, g], rs_send.at[d - 1, g], rs_recv.at[d - 1, g], {"feature": to})

    shape = (rows, count * quarter)
    column = lax.broadcasted_iota(jnp.int32, shape, 1)
    key_pos = lax.shift_right_logical(column, 6) * rows + f * quarter + jnp.bitwise_and(column, quarter - 1)
    query_pos = s * rows + lax.broadcasted_iota(jnp.int32, shape, 0)
    allowed = key_pos <= query_pos
    diagonal = lax.broadcasted_iota(jnp.int32, (quarter, hd), 0) == lax.broadcasted_iota(jnp.int32, (quarter, hd), 1)

    def head(g, carry):
        scores = dot_nt(qcat[g], kcat[...]) + dot_nt(qcat[g, :, :hd], klow[...])
        squared = jnp.where(allowed, scores * scores, 0.0)
        ph, plow = halves(squared)
        both = dot(ph, vcat[...])
        numerator = both[:, :hd] + both[:, hd:] + dot(plow, vcat[:, :hd])
        denominator = jnp.sum(squared, axis=1, keepdims=True)
        for p in range(parts):
            part = slice(p * quarter, (p + 1) * quarter)
            rs_src[g, p, :quarter] = numerator[part]
            spread = jnp.where(diagonal, jnp.broadcast_to(denominator[part], (quarter, hd)), 0.0)
            line = jnp.sum(spread, axis=0, keepdims=True)
            rs_src[g, p, quarter:] = jnp.broadcast_to(line, (8, hd))
        for d in range(1, parts):
            rs_copy(d, g).start()
        return carry

    lax.fori_loop(0, group, head, 0)

    w_takes[0].wait_recv()
    w_takes[1].wait_recv()
    w_steps[2].start()
    w_steps[3].start()

    def a_copy(i, g, slot, where):
        return remote(abuf.at[slot, g], abuf.at[slot, g], a_send.at[i, g], a_recv.at[i, g], {"seq": where})

    def normalize(g, carry):
        for d in range(1, parts):
            rs_copy(d, g).wait_recv()
        total = rs_src[g, f] + rs_rcv[0, g]
        for d in range(1, parts - 1):
            total = total + rs_rcv[d, g]
        line = jnp.broadcast_to(total[quarter:quarter + 1], (quarter, hd))
        denominator = jnp.sum(jnp.where(diagonal, line, 0.0), axis=1, keepdims=True)
        abuf[s, g] = total[:quarter] / (denominator + 1.0)
        a_copy(0, g, s, right).start()
        a_copy(half, g, s, left).start()
        return carry

    lax.fori_loop(0, group, normalize, 0)

    w_takes[2].wait_recv()
    w_takes[3].wait_recv()
    for p in range(parts):
        high, low = halves(wt[p])
        wh[p * hd:(p + 1) * hd] = high[:hd]
        wl[p * hd:(p + 1) * hd] = low[:hd]
        wh[parts * hd + p * rest:parts * hd + (p + 1) * rest] = high[hd:]
        wl[parts * hd + p * rest:parts * hd + (p + 1) * rest] = low[hd:]

    lane_group = lax.div(lax.broadcasted_iota(jnp.int32, (quarter // parts, hd), 1), rest)
    sub = quarter // parts

    def c1_copy(i, p, where, j):
        return remote(cpk.at[i, p], c1r.at[j, k], c1_send.at[i, p], c1_recv.at[j, k], {"kvhead": where})

    def c1_each(i, act):
        h, j = lax.div(i, half), lax.rem(i, half)
        for d in range(1, parts):
            p = lax.rem(y + d, parts)
            act(c1_copy(i, p, 2 * p + h, j))

        @pl.when(h != c)
        def _():
            act(c1_copy(i, y, twin, j))

    def project(slots):
        a = jnp.concatenate(
            [jnp.concatenate([abuf[i, g] for g in range(group)], axis=1) for i in slots], axis=0
        )
        n = len(slots) * quarter
        high, low = halves(a)
        both = dot_nt(jnp.concatenate([high, low], axis=0), wh[...])
        out = both[:n] + both[n:] + dot_nt(high, wl[...])
        for m, i in enumerate(slots):
            block = out[m * quarter:(m + 1) * quarter]
            tail = block[:, parts * hd:]
            for p in range(parts):
                cpk[i, p, :quarter] = block[:, p * hd:(p + 1) * hd]
                packed = jnp.zeros((sub, hd), F32)
                for g in range(parts):
                    piece = tail[g * sub:(g + 1) * sub]
                    shift = (rest * (g - p)) % hd
                    if shift:
                        piece = pltpu.roll(piece, shift, 1)
                    packed = jnp.where(lane_group == g, piece, packed)
                cpk[i, p, quarter:] = packed
            c1_each(i, lambda copy: copy.start())

    project([s])

    def step(t, carry):
        for g in range(group):
            a_copy(t - 1, g, at_z(-t), right).wait_recv()
            a_copy(t, g, at_z(-t), right).start()
            a_copy(half + t - 1, g, at_z(t), left).wait_recv()

            @pl.when(t < half - 1)
            def _():
                a_copy(half + t, g, at_z(t), left).start()

        project([at_z(-t), at_z(t)])
        return carry

    lax.fori_loop(1, half, step, 0)
    for g in range(group):
        a_copy(half - 1, g, at_z(-half), right).wait_recv()
    project([at_z(-half)])

    def c2_copy(j, to):
        slot = lax.rem(s, half)
        return remote(red.at[j], c2r.at[slot], c2_send.at[j], c2_recv.at[slot], {"kvhead": 2 * y + seq_half, "seq": to})

    def reduce(j, carry):
        i = half * c + j
        total = cpk[i, y]
        for d in range(1, heads):
            other = lax.rem(k + d, heads)
            remote(cpk.at[i, y], c1r.at[j, other], c1_send.at[i, y], c1_recv.at[j, other], {"kvhead": twin}).wait_recv()
            total = total + c1r[j, other]

        @pl.when(i == s)
        def _():
            c2r[j] = total

        @pl.when(i != s)
        def _():
            red[j] = total
            c2_copy(j, i).start()

        return carry

    lax.fori_loop(0, half, reduce, 0)

    def arrive(j, carry):
        @pl.when(half * c + j != s)
        def _():
            remote(red.at[j], c2r.at[j], c2_send.at[j], c2_recv.at[j], {"kvhead": twin}).wait_recv()

        return carry

    lax.fori_loop(0, half, arrive, 0)

    lane = lax.broadcasted_iota(jnp.int32, (quarter, hd), 1)
    for tile in range(parts + 1):
        value = None
        if tile < parts:
            value = c2r[tile, :quarter]
            if tile:
                value = pltpu.roll(value, rest * tile, 1)
        if tile > 0:
            j = tile - 1
            before = c2r[j, :quarter]
            if j:
                before = pltpu.roll(before, rest * j, 1)
            packed = c2r[j, quarter:]
            tail = jnp.concatenate(
                [pltpu.roll(packed, (rest * (j - g)) % hd, 1) if (j - g) % parts else packed for g in range(parts)], axis=0
            )
            value = tail if value is None else jnp.where(lane < rest * tile, tail, value)
            if j:
                value = jnp.where(lane < rest * j, before, value)
        o_ref[:, tile * hd:(tile + 1) * hd] = value

    for t in range(half):
        kv_fwd(t).wait_send()
        if t < half - 1:
            kv_bwd(t).wait_send()
    for copy in w_steps:
        copy.wait_send()

    def drain(g, carry):
        for d in range(1, parts):
            rs_copy(d, g).wait_send()
        for t in range(half):
            a_copy(t, g, at_z(-t), right).wait_send()
            if t < half - 1:
                a_copy(half + t, g, at_z(t), left).wait_send()
        return carry

    lax.fori_loop(0, group, drain, 0)

    def drain_c1(i, carry):
        c1_each(i, lambda copy: copy.wait_send())
        return carry

    lax.fori_loop(0, count, drain_c1, 0)

    def drain_c2(j, carry):
        @pl.when(half * c + j != s)
        def _():
            c2_copy(j, half * c + j).wait_send()

        return carry

    lax.fori_loop(0, half, drain_c2, 0)


def local(queries, keys, values, w_out, *, parts, count, heads):
    rows, group, hd = queries.shape
    quarter = rows // parts
    depth, wide = w_out.shape
    half = count // 2
    packed = quarter * wide // hd
    columns = parts * wide
    keys_all = count * quarter
    dma = pltpu.SemaphoreType.DMA
    any_space = pl.BlockSpec(memory_space=pl.ANY)
    return pl.pallas_call(
        kernel,
        out_shape=jax.ShapeDtypeStruct((quarter, half * wide), F32),
        in_specs=[any_space] * 4,
        out_specs=pl.BlockSpec(memory_space=pltpu.VMEM),
        scratch_shapes=[
            pltpu.VMEM((group, rows, hd), F32),
            pltpu.VMEM((count, 2, quarter, hd), F32),
            pltpu.VMEM((parts, wide, depth), F32),
            pltpu.VMEM((group, rows, 2 * hd), BF16),
            pltpu.VMEM((keys_all, 2 * hd), BF16),
            pltpu.VMEM((keys_all, hd), BF16),
            pltpu.VMEM((keys_all, 2 * hd), BF16),
            pltpu.VMEM((group, parts, quarter + 8, hd), F32),
            pltpu.VMEM((parts - 1, group, quarter + 8, hd), F32),
            pltpu.VMEM((count, group, quarter, hd), F32),
            pltpu.VMEM((columns, depth), BF16),
            pltpu.VMEM((columns, depth), BF16),
            pltpu.VMEM((count, parts, packed, hd), F32),
            pltpu.VMEM((half, heads, packed, hd), F32),
            pltpu.VMEM((half, packed, hd), F32),
            pltpu.VMEM((half, packed, hd), F32),
            dma((4,)),
            dma((count - 1,)),
            dma((count - 1,)),
            dma((4,)),
            dma((4,)),
            dma((parts - 1, group)),
            dma((parts - 1, group)),
            dma((count - 1, group)),
            dma((count - 1, group)),
            dma((count, parts)),
            dma((half, heads)),
            dma((half,)),
            dma((half,)),
        ],
        compiler_params=pltpu.CompilerParams(
            collective_id=0, has_side_effects=True, vmem_limit_bytes=60 * 1024 * 1024
        ),
        name="power_attention",
    )(
        jnp.transpose(queries, (1, 0, 2)),
        keys.reshape(rows, hd),
        values.reshape(rows, hd),
        w_out.T,
    )


def solution(mesh):
    body = functools.partial(
        local, parts=mesh.shape["feature"], count=mesh.shape["seq"], heads=mesh.shape["kvhead"]
    )
    in_specs = (
        P("seq", "kvhead", None),
        P("seq", "kvhead", None),
        P("seq", "kvhead", None),
        P("kvhead", ("feature", "seq")),
    )
    out_specs = P(("seq", "feature"), "kvhead")
    return jax.shard_map(body, mesh=mesh, in_specs=in_specs, out_specs=out_specs, check_vma=False)
```

```python
import functools

import jax
import jax.numpy as jnp
from jax import lax
from jax.experimental import pallas as pl
from jax.experimental.pallas import tpu as pltpu
from jax.sharding import PartitionSpec as P

MESH = pl.DeviceIdType.MESH
NT = (((1,), (1,)), ((), ()))
F32 = jnp.float32
BF16 = jnp.bfloat16


def halves(x):
    high = x.astype(BF16)
    return high, (x - high.astype(F32)).astype(BF16)


def dot(a, b):
    return jnp.dot(a, b, preferred_element_type=F32)


def dot_nt(a, b):
    return lax.dot_general(a, b, NT, preferred_element_type=F32)


def kernel(
    q_hbm, k_hbm, v_hbm, w_hbm, o_ref,
    qv, kv, wt, qcat, kcat, klow, vcat, rs_src, rs_rcv, abuf, wh, wl, cpk, c0r, c1r, red, c2r,
    load_sem, kv_send, kv_recv, w_send, w_recv, rs_send, rs_recv, a_send, a_recv,
    c0_send, c0_recv, c1_send, c1_recv, c2_send, c2_recv,
):
    group, rows, hd = q_hbm.shape
    parts = wt.shape[0]
    count = kv.shape[0]
    heads = 2 * parts
    quarter = rows // parts
    half = count // 2
    wide = w_hbm.shape[0]
    rest = wide - hd
    lanes = hd // parts
    f = lax.axis_index("feature")
    k = lax.axis_index("kvhead")
    s = lax.axis_index("seq")
    y, c = lax.div(k, 2), lax.rem(k, 2)
    twin = k + 1 - 2 * c
    seq_half = lax.div(s, half)

    def at_z(d):
        return lax.rem(s + d + count, count)

    def at_x(d):
        return lax.rem(f + d + parts, parts)

    right, left = at_z(1), at_z(-1)

    own = pl.ds(pl.multiple_of(f * quarter, quarter), quarter)
    loads = [
        pltpu.make_async_copy(w_hbm, wt.at[f], load_sem.at[0]),
        pltpu.make_async_copy(k_hbm.at[own], kv.at[s, 0], load_sem.at[1]),
        pltpu.make_async_copy(v_hbm.at[own], kv.at[s, 1], load_sem.at[2]),
        pltpu.make_async_copy(q_hbm, qv, load_sem.at[3]),
    ]
    for load in loads:
        load.start()

    barrier = pltpu.get_barrier_semaphore()
    peers = 0
    for d in range(1, parts):
        pl.semaphore_signal(barrier, inc=1, device_id={"feature": at_x(d)}, device_id_type=MESH)
        peers += 1
    for d in range(1, count):
        pl.semaphore_signal(barrier, inc=1, device_id={"seq": at_z(d)}, device_id_type=MESH)
        pl.semaphore_signal(barrier, inc=1, device_id={"kvhead": twin, "seq": at_z(d)}, device_id_type=MESH)
        peers += 2
    for d in range(1, heads):
        pl.semaphore_signal(barrier, inc=1, device_id={"kvhead": lax.rem(k + d, heads)}, device_id_type=MESH)
        peers += 1
    loads[1].wait()
    loads[2].wait()
    pl.semaphore_wait(barrier, peers)

    def remote(src, dst, send, recv, where):
        return pltpu.make_async_remote_copy(
            src_ref=src, dst_ref=dst, send_sem=send, recv_sem=recv, device_id=where, device_id_type=MESH
        )

    pieces = 4
    piece = 2 * quarter // pieces
    hops = (2, -2, 1, -1, 3, -3, 4)

    def kv_copy(i, n, slot, where):
        ref = kv.at[slot, n * piece // quarter, pl.ds(n * piece % quarter, piece)]
        return remote(ref, ref, kv_send.at[i, n], kv_recv.at[i, n], {"seq": where})

    def kv_from(i, n):
        return kv_copy(i, n, at_z(-hops[i]), right)

    def kv_out(i, n):
        if i < 4:
            return kv_copy(i, n, s, at_z(hops[i]))
        if i < 6:
            step = 2 if i == 4 else -2
            return kv_copy(i, n, at_z(-step), at_z(step // 2))
        step = 2 if n < pieces // 2 else -2
        return kv_copy(i, n, at_z(-step), at_z(step))

    def kv_take(slot):
        place = pl.ds(pl.multiple_of(slot * quarter, quarter), quarter)
        kh, kl = halves(kv[slot, 0])
        vh, vl = halves(kv[slot, 1])
        kcat[place, :hd] = kh
        kcat[place, hd:] = kh
        klow[place, :] = kl
        vcat[place, :hd] = vh
        vcat[place, hd:] = vl

    for i in range(4):
        for n in range(pieces):
            kv_out(i, n).start()

    def w_copy(i, src, where):
        return remote(src, src, w_send.at[i], w_recv.at[i], {"feature": where})

    w_top, w_low = pl.ds(0, wide // 2), pl.ds(wide // 2, wide // 2)
    w_steps = [
        w_copy(0, wt.at[f], at_x(1)),
        w_copy(1, wt.at[f], at_x(-1)),
        w_copy(2, wt.at[at_x(-1), w_top], at_x(1)),
        w_copy(3, wt.at[at_x(1), w_low], at_x(-1)),
    ]
    w_takes = [
        w_copy(0, wt.at[at_x(-1)], at_x(1)),
        w_copy(1, wt.at[at_x(1)], at_x(-1)),
        w_copy(2, wt.at[at_x(2), w_top], at_x(1)),
        w_copy(3, wt.at[at_x(2), w_low], at_x(-1)),
    ]
    loads[0].wait()
    w_steps[0].start()
    w_steps[1].start()

    loads[3].wait()
    for g in range(group):
        qh, ql = halves(qv[g] * (hd ** -0.5))
        qcat[g, :, :hd] = qh
        qcat[g, :, hd:] = ql
    kv_take(s)
    for n in range(pieces):
        kv_from(0, n).wait_recv()
        kv_out(4, n).start()
        if n < pieces // 2:
            kv_out(6, n).start()
        kv_from(1, n).wait_recv()
        kv_out(5, n).start()
        if n >= pieces // 2:
            kv_out(6, n).start()
    kv_take(at_z(-2))
    kv_take(at_z(2))
    for i in range(2, len(hops)):
        for n in range(pieces):
            kv_from(i, n).wait_recv()
        kv_take(at_z(-hops[i]))

    def rs_copy(d, g):
        to = at_x(d)
        return remote(rs_src.at[g, to], rs_rcv.at[d - 1, g], rs_send.at[d - 1, g], rs_recv.at[d - 1, g], {"feature": to})

    shape = (rows, count * quarter)
    column = lax.broadcasted_iota(jnp.int32, shape, 1)
    key_pos = lax.shift_right_logical(column, 6) * rows + f * quarter + jnp.bitwise_and(column, quarter - 1)
    query_pos = s * rows + lax.broadcasted_iota(jnp.int32, shape, 0)
    allowed = key_pos <= query_pos
    diagonal = lax.broadcasted_iota(jnp.int32, (quarter, hd), 0) == lax.broadcasted_iota(jnp.int32, (quarter, hd), 1)

    def head(g, carry):
        scores = dot_nt(qcat[g], kcat[...]) + dot_nt(qcat[g, :, :hd], klow[...])
        squared = jnp.where(allowed, scores * scores, 0.0)
        ph, plow = halves(squared)
        both = dot(ph, vcat[...])
        numerator = both[:, :hd] + both[:, hd:] + dot(plow, vcat[:, :hd])
        denominator = jnp.sum(squared, axis=1, keepdims=True)
        for p in range(parts):
            part = slice(p * quarter, (p + 1) * quarter)
            rs_src[g, p, :quarter] = numerator[part]
            spread = jnp.where(diagonal, jnp.broadcast_to(denominator[part], (quarter, hd)), 0.0)
            line = jnp.sum(spread, axis=0, keepdims=True)
            rs_src[g, p, quarter:] = jnp.broadcast_to(line, (8, hd))
        for d in range(1, parts):
            rs_copy(d, g).start()
        return carry

    lax.fori_loop(0, group, head, 0)

    def a_copy(i, g, slot, where):
        return remote(abuf.at[slot, g], abuf.at[slot, g], a_send.at[i, g], a_recv.at[i, g], {"seq": where})

    def normalize(g):
        for d in range(1, parts):
            rs_copy(d, g).wait_recv()
        total = rs_src[g, f] + rs_rcv[0, g]
        for d in range(1, parts - 1):
            total = total + rs_rcv[d, g]
        line = jnp.broadcast_to(total[quarter:quarter + 1], (quarter, hd))
        denominator = jnp.sum(jnp.where(diagonal, line, 0.0), axis=1, keepdims=True)
        abuf[s, g] = total[:quarter] / (denominator + 1.0)
        a_copy(0, g, s, right).start()
        a_copy(half, g, s, left).start()

    def relay(t, g):
        a_copy(t - 1, g, at_z(-t), right).wait_recv()
        if t < half:
            a_copy(t, g, at_z(-t), right).start()
            a_copy(half + t - 1, g, at_z(t), left).wait_recv()
            if t < half - 1:
                a_copy(half + t, g, at_z(t), left).start()

    def split_weights(p):
        high, low = halves(wt[p])
        main = pl.ds(pl.multiple_of(p * hd, hd), hd)
        tail = pl.ds(pl.multiple_of(parts * hd + p * rest, rest), rest)
        wh[main, :] = high[:hd]
        wl[main, :] = low[:hd]
        wh[tail, :] = high[hd:]
        wl[tail, :] = low[hd:]

    lane_group = lax.div(lax.broadcasted_iota(jnp.int32, (quarter // parts, hd), 1), rest)
    sub = quarter // parts

    def c0_copy(i):
        j = lax.rem(i, half)
        return remote(cpk.at[i], c0r.at[j], c0_send.at[i], c0_recv.at[j], {"kvhead": twin})

    def c1_copy(i, d):
        p = lax.rem(y + d, parts)
        j = lax.rem(i, half)
        return remote(cpk.at[i, p], c1r.at[j, d - 1], c1_send.at[j, d - 1], c1_recv.at[j, d - 1], {"kvhead": 2 * p + c})

    def c2_copy(i):
        j, slot = lax.rem(i, half), lax.rem(s, half)
        return remote(red.at[j], c2r.at[slot], c2_send.at[j], c2_recv.at[slot], {"kvhead": 2 * y + seq_half, "seq": i})

    def mine(i):
        return lax.div(i, half) == c

    def merge(slots):
        for i in slots:
            @pl.when(mine(i))
            def _():
                c0_copy(i).wait_recv()
                for p in range(parts):
                    cpk[i, p] = cpk[i, p] + c0r[lax.rem(i, half), p]
                for d in range(1, parts):
                    c1_copy(i, d).start()

    def finish(slots):
        for i in slots:
            @pl.when(mine(i))
            def _():
                j = lax.rem(i, half)
                total = cpk[i, y]
                for d in range(1, parts):
                    c1_copy(i, d).wait_recv()
                    total = total + c1r[j, d - 1]

                @pl.when(i == s)
                def _():
                    c2r[j] = total

                @pl.when(i != s)
                def _():
                    red[j] = total
                    c2_copy(i).start()

    def project(slots):
        a = jnp.concatenate(
            [jnp.concatenate([abuf[i, g] for g in range(group)], axis=1) for i in slots], axis=0
        )
        n = len(slots) * quarter
        high, low = halves(a)
        both = dot_nt(jnp.concatenate([high, low], axis=0), wh[...])
        out = both[:n] + both[n:] + dot_nt(high, wl[...])
        for m, i in enumerate(slots):
            block = out[m * quarter:(m + 1) * quarter]
            tail = block[:, parts * hd:]
            for p in range(parts):
                cpk[i, p, :quarter] = block[:, p * hd:(p + 1) * hd]
                packed = jnp.zeros((sub, hd), F32)
                for g in range(parts):
                    piece = tail[g * sub:(g + 1) * sub]
                    shift = (rest * (g - p)) % hd
                    if shift:
                        piece = pltpu.roll(piece, shift, 1)
                    packed = jnp.where(lane_group == g, piece, packed)
                cpk[i, p, quarter:] = packed

            @pl.when(jnp.logical_not(mine(i)))
            def _():
                c0_copy(i).start()


    steps = [[s]] + [[at_z(-t), at_z(t)] for t in range(1, half)] + [[at_z(-half)]]
    w_takes[0].wait_recv()
    w_takes[1].wait_recv()
    w_steps[2].start()
    w_steps[3].start()
    normalize(0)
    for p in (0, -1, 1):
        split_weights(at_x(p))
    normalize(1)
    relay(1, 0)
    normalize(2)
    relay(1, 1)
    normalize(3)
    relay(1, 2)
    relay(2, 0)
    normalize(4)
    relay(1, 3)
    relay(2, 1)
    w_takes[2].wait_recv()
    w_takes[3].wait_recv()
    split_weights(at_x(2))
    project(steps[0])
    relay(1, 4)
    relay(2, 2)
    relay(3, 0)
    relay(2, 3)
    relay(3, 1)
    project(steps[1])
    relay(2, 4)
    relay(3, 2)
    relay(3, 3)
    project(steps[2])
    relay(3, 4)
    for g in range(group - 1):
        relay(half, g)
    project(steps[3])
    merge(steps[0])
    merge(steps[1])
    relay(half, group - 1)
    project(steps[4])
    merge(steps[2])
    merge(steps[3])
    merge(steps[4])
    finish(steps[0])
    finish(steps[1])
    finish(steps[2])
    finish(steps[3])
    finish(steps[4])

    def arrive(j, carry):
        @pl.when(half * c + j != s)
        def _():
            remote(red.at[j], c2r.at[j], c2_send.at[j], c2_recv.at[j], {"kvhead": twin}).wait_recv()

        return carry

    lax.fori_loop(0, half, arrive, 0)

    lane = lax.broadcasted_iota(jnp.int32, (quarter, hd), 1)
    for tile in range(parts + 1):
        value = None
        if tile < parts:
            value = c2r[tile, :quarter]
            if tile:
                value = pltpu.roll(value, rest * tile, 1)
        if tile > 0:
            j = tile - 1
            before = c2r[j, :quarter]
            if j:
                before = pltpu.roll(before, rest * j, 1)
            packed = c2r[j, quarter:]
            tail = jnp.concatenate(
                [pltpu.roll(packed, (rest * (j - g)) % hd, 1) if (j - g) % parts else packed for g in range(parts)], axis=0
            )
            value = tail if value is None else jnp.where(lane < rest * tile, tail, value)
            if j:
                value = jnp.where(lane < rest * j, before, value)
        o_ref[:, tile * hd:(tile + 1) * hd] = value

    for i in range(len(hops)):
        for n in range(pieces):
            kv_out(i, n).wait_send()
    for copy in w_steps:
        copy.wait_send()

    def drain(g, carry):
        for d in range(1, parts):
            rs_copy(d, g).wait_send()
        for t in range(half):
            a_copy(t, g, at_z(-t), right).wait_send()
            if t < half - 1:
                a_copy(half + t, g, at_z(t), left).wait_send()
        return carry

    lax.fori_loop(0, group, drain, 0)

    def drain_c(i, carry):
        @pl.when(mine(i))
        def _():
            for d in range(1, parts):
                c1_copy(i, d).wait_send()

            @pl.when(i != s)
            def _():
                c2_copy(i).wait_send()

        @pl.when(jnp.logical_not(mine(i)))
        def _():
            c0_copy(i).wait_send()

        return carry

    lax.fori_loop(0, count, drain_c, 0)


def local(queries, keys, values, w_out, *, parts, count):
    rows, group, hd = queries.shape
    quarter = rows // parts
    depth, wide = w_out.shape
    half = count // 2
    packed = quarter * wide // hd
    columns = parts * wide
    keys_all = count * quarter
    dma = pltpu.SemaphoreType.DMA
    any_space = pl.BlockSpec(memory_space=pl.ANY)
    return pl.pallas_call(
        kernel,
        out_shape=pltpu.VMEM((quarter, half * wide), F32),
        in_specs=[any_space] * 4,
        out_specs=pl.BlockSpec(memory_space=pltpu.VMEM),
        scratch_shapes=[
            pltpu.VMEM((group, rows, hd), F32),
            pltpu.VMEM((count, 2, quarter, hd), F32),
            pltpu.VMEM((parts, wide, depth), F32),
            pltpu.VMEM((group, rows, 2 * hd), BF16),
            pltpu.VMEM((keys_all, 2 * hd), BF16),
            pltpu.VMEM((keys_all, hd), BF16),
            pltpu.VMEM((keys_all, 2 * hd), BF16),
            pltpu.VMEM((group, parts, quarter + 8, hd), F32),
            pltpu.VMEM((parts - 1, group, quarter + 8, hd), F32),
            pltpu.VMEM((count, group, quarter, hd), F32),
            pltpu.VMEM((columns, depth), BF16),
            pltpu.VMEM((columns, depth), BF16),
            pltpu.VMEM((count, parts, packed, hd), F32),
            pltpu.VMEM((half, parts, packed, hd), F32),
            pltpu.VMEM((half, parts - 1, packed, hd), F32),
            pltpu.VMEM((half, packed, hd), F32),
            pltpu.VMEM((half, packed, hd), F32),
            dma((4,)),
            dma((count - 1, 4)),
            dma((count - 1, 4)),
            dma((4,)),
            dma((4,)),
            dma((parts - 1, group)),
            dma((parts - 1, group)),
            dma((count - 1, group)),
            dma((count - 1, group)),
            dma((count,)),
            dma((half,)),
            dma((half, parts - 1)),
            dma((half, parts - 1)),
            dma((half,)),
            dma((half,)),
        ],
        compiler_params=pltpu.CompilerParams(
            collective_id=0, has_side_effects=True, vmem_limit_bytes=60 * 1024 * 1024
        ),
        name="power_attention",
    )(
        jnp.transpose(queries, (1, 0, 2)),
        keys.reshape(rows, hd),
        values.reshape(rows, hd),
        w_out.T,
    )


def solution(mesh):
    body = functools.partial(
        local, parts=mesh.shape["feature"], count=mesh.shape["seq"]
    )
    in_specs = (
        P("seq", "kvhead", None),
        P("seq", "kvhead", None),
        P("seq", "kvhead", None),
        P("kvhead", ("feature", "seq")),
    )
    out_specs = P(("seq", "feature"), "kvhead")
    return jax.shard_map(body, mesh=mesh, in_specs=in_specs, out_specs=out_specs, check_vma=False)
```

```python
import functools

import jax
import jax.numpy as jnp
from jax import lax
from jax.experimental import pallas as pl
from jax.experimental.pallas import tpu as pltpu
from jax.sharding import PartitionSpec as P

MESH = pl.DeviceIdType.MESH
NT = (((1,), (1,)), ((), ()))
F32 = jnp.float32
BF16 = jnp.bfloat16


def halves(x):
    high = x.astype(BF16)
    return high, (x - high.astype(F32)).astype(BF16)


def dot(a, b):
    return jnp.dot(a, b, preferred_element_type=F32)


def dot_nt(a, b):
    return lax.dot_general(a, b, NT, preferred_element_type=F32)


def kernel(
    q_hbm, k_hbm, v_hbm, w_hbm, o_ref,
    qv, kv, wt, qcat, kcat, klow, vcat, rs_src, rs_rcv, den_src, den_rcv, abuf, wh, wl, cpk, c0r, c1r, red, c2r,
    load_sem, kv_send, kv_recv, w_send, w_recv, rs_send, rs_recv, den_send, den_recv, a_send, a_recv,
    c0_send, c0_recv, c1_send, c1_recv, c2_send, c2_recv,
):
    group, rows, hd = q_hbm.shape
    parts = wt.shape[0]
    count = kv.shape[0]
    heads = 2 * parts
    quarter = rows // parts
    half = count // 2
    wide = w_hbm.shape[0]
    rest = wide - hd
    lanes = hd // parts
    f = lax.axis_index("feature")
    k = lax.axis_index("kvhead")
    s = lax.axis_index("seq")
    y, c = lax.div(k, 2), lax.rem(k, 2)
    twin = k + 1 - 2 * c
    seq_half = lax.div(s, half)

    def at_z(d):
        return lax.rem(s + d + count, count)

    def at_x(d):
        return lax.rem(f + d + parts, parts)

    right, left = at_z(1), at_z(-1)

    own = pl.ds(pl.multiple_of(f * quarter, quarter), quarter)
    loads = [
        pltpu.make_async_copy(w_hbm, wt.at[f], load_sem.at[0]),
        pltpu.make_async_copy(k_hbm.at[own], kv.at[s, 0], load_sem.at[1]),
        pltpu.make_async_copy(v_hbm.at[own], kv.at[s, 1], load_sem.at[2]),
        pltpu.make_async_copy(q_hbm, qv, load_sem.at[3]),
    ]
    for load in loads:
        load.start()

    barrier = pltpu.get_barrier_semaphore()
    peers = 0
    for d in range(1, parts):
        pl.semaphore_signal(barrier, inc=1, device_id={"feature": at_x(d)}, device_id_type=MESH)
        peers += 1
    for d in range(1, count):
        pl.semaphore_signal(barrier, inc=1, device_id={"seq": at_z(d)}, device_id_type=MESH)
        pl.semaphore_signal(barrier, inc=1, device_id={"kvhead": twin, "seq": at_z(d)}, device_id_type=MESH)
        peers += 2
    for d in range(1, heads):
        pl.semaphore_signal(barrier, inc=1, device_id={"kvhead": lax.rem(k + d, heads)}, device_id_type=MESH)
        peers += 1
    loads[1].wait()
    loads[2].wait()
    pl.semaphore_wait(barrier, peers)

    def remote(src, dst, send, recv, where):
        return pltpu.make_async_remote_copy(
            src_ref=src, dst_ref=dst, send_sem=send, recv_sem=recv, device_id=where, device_id_type=MESH
        )

    pieces = 4
    piece = 2 * quarter // pieces
    hops = (2, -2, 1, -1, 3, -3, 4)

    def kv_copy(i, n, slot, where):
        ref = kv.at[slot, n * piece // quarter, pl.ds(n * piece % quarter, piece)]
        return remote(ref, ref, kv_send.at[i, n], kv_recv.at[i, n], {"seq": where})

    def kv_from(i, n):
        return kv_copy(i, n, at_z(-hops[i]), right)

    def kv_out(i, n):
        if i < 4:
            return kv_copy(i, n, s, at_z(hops[i]))
        if i < 6:
            step = 2 if i == 4 else -2
            return kv_copy(i, n, at_z(-step), at_z(step // 2))
        step = 2 if n < pieces // 2 else -2
        return kv_copy(i, n, at_z(-step), at_z(step))

    def kv_take(slot):
        place = pl.ds(pl.multiple_of(slot * quarter, quarter), quarter)
        kh, kl = halves(kv[slot, 0])
        vh, vl = halves(kv[slot, 1])
        kcat[place, :hd] = kh
        kcat[place, hd:] = kh
        klow[place, :] = kl
        vcat[place, :hd] = vh
        vcat[place, hd:] = vl

    for i in range(4):
        for n in range(pieces):
            kv_out(i, n).start()

    def w_copy(i, src, where):
        return remote(src, src, w_send.at[i], w_recv.at[i], {"feature": where})

    w_top, w_low = pl.ds(0, wide // 2), pl.ds(wide // 2, wide // 2)
    w_steps = [
        w_copy(0, wt.at[f], at_x(1)),
        w_copy(1, wt.at[f], at_x(-1)),
        w_copy(2, wt.at[at_x(-1), w_top], at_x(1)),
        w_copy(3, wt.at[at_x(1), w_low], at_x(-1)),
    ]
    w_takes = [
        w_copy(0, wt.at[at_x(-1)], at_x(1)),
        w_copy(1, wt.at[at_x(1)], at_x(-1)),
        w_copy(2, wt.at[at_x(2), w_top], at_x(1)),
        w_copy(3, wt.at[at_x(2), w_low], at_x(-1)),
    ]
    loads[0].wait()
    w_steps[0].start()
    w_steps[1].start()

    loads[3].wait()
    for g in range(group):
        qh, ql = halves(qv[g] * (hd ** -0.5))
        qcat[g, :, :hd] = qh
        qcat[g, :, hd:] = ql
    kv_take(s)
    for n in range(pieces):
        kv_from(0, n).wait_recv()
        kv_out(4, n).start()
        if n < pieces // 2:
            kv_out(6, n).start()
        kv_from(1, n).wait_recv()
        kv_out(5, n).start()
        if n >= pieces // 2:
            kv_out(6, n).start()
    kv_take(at_z(-2))
    kv_take(at_z(2))
    for i in range(2, len(hops)):
        for n in range(pieces):
            kv_from(i, n).wait_recv()
        kv_take(at_z(-hops[i]))

    def rs_copy(d, g):
        to = at_x(d)
        return remote(rs_src.at[g, to], rs_rcv.at[d - 1, g], rs_send.at[d - 1, g], rs_recv.at[d - 1, g], {"feature": to})

    def den_copy(d, g):
        to = at_x(d)
        return remote(
            den_src.at[g, to], den_rcv.at[d - 1, g], den_send.at[d - 1, g], den_recv.at[d - 1, g], {"feature": to}
        )

    shape = (rows, count * quarter)
    column = lax.broadcasted_iota(jnp.int32, shape, 1)
    key_pos = lax.shift_right_logical(column, 6) * rows + f * quarter + jnp.bitwise_and(column, quarter - 1)
    query_pos = s * rows + lax.broadcasted_iota(jnp.int32, shape, 0)
    allowed = key_pos <= query_pos
    diagonal = lax.broadcasted_iota(jnp.int32, (quarter, hd), 0) == lax.broadcasted_iota(jnp.int32, (quarter, hd), 1)

    def head(g, carry):
        scores = dot_nt(qcat[g], kcat[...]) + dot_nt(qcat[g, :, :hd], klow[...])
        squared = jnp.where(allowed, scores * scores, 0.0)
        ph, plow = halves(squared)
        both = dot(ph, vcat[...])
        numerator = both[:, :hd] + both[:, hd:] + dot(plow, vcat[:, :hd])
        denominator = jnp.sum(squared, axis=1, keepdims=True)
        for p in range(parts):
            part = slice(p * quarter, (p + 1) * quarter)
            rs_src[g, p] = numerator[part]
            spread = jnp.where(diagonal, jnp.broadcast_to(denominator[part], (quarter, hd)), 0.0)
            den_src[g, p] = jnp.sum(spread, axis=0, keepdims=True)
        for d in range(1, parts):
            den_copy(d, g).start()
            rs_copy(d, g).start()
        return carry

    lax.fori_loop(0, group, head, 0)

    def a_copy(i, g, slot, where):
        return remote(abuf.at[slot, g], abuf.at[slot, g], a_send.at[i, g], a_recv.at[i, g], {"seq": where})

    ringed = 2

    def normalize(g):
        for d in range(1, parts):
            den_copy(d, g).wait_recv()
            rs_copy(d, g).wait_recv()
        total = rs_src[g, f] + rs_rcv[0, g]
        line = den_src[g, f] + den_rcv[0, g]
        for d in range(1, parts - 1):
            total = total + rs_rcv[d, g]
            line = line + den_rcv[d, g]
        line = jnp.broadcast_to(line, (quarter, hd))
        denominator = jnp.sum(jnp.where(diagonal, line, 0.0), axis=1, keepdims=True)
        abuf[s, g] = total / (denominator + 1.0)
        if g < ringed:
            a_copy(0, g, s, right).start()
            a_copy(half, g, s, left).start()
        else:
            for i in range(4):
                a_out(i, g).start()

    def a_last(g):
        if g % 2 == 0:
            return a_copy(half - 1, g, at_z(1 - half), right)
        return a_copy(half - 1, g, at_z(half - 1), left)

    def relay(t, g):
        a_copy(t - 1, g, at_z(-t), right).wait_recv()
        if t < half:
            a_copy(half + t - 1, g, at_z(t), left).wait_recv()
        if t < half - 1:
            a_copy(t, g, at_z(-t), right).start()
            a_copy(half + t, g, at_z(t), left).start()
        if t == half - 1:
            a_last(g).start()

    def a_from(i, g):
        return a_copy(i, g, at_z(-hops[i]), right)

    def a_out(i, g):
        if i < 4:
            return a_copy(i, g, s, at_z(hops[i]))
        if i < 6:
            step = 2 if i == 4 else -2
            return a_copy(i, g, at_z(-step), at_z(step // 2))
        step = 2 if g % 2 == 0 else -2
        return a_copy(i, g, at_z(-step), at_z(step))

    def forward(g):
        a_from(0, g).wait_recv()
        if g % 2 == 0:
            a_out(6, g).start()
        a_out(4, g).start()
        a_from(1, g).wait_recv()
        if g % 2 == 1:
            a_out(6, g).start()
        a_out(5, g).start()

    def arrived(*distances):
        for g in range(ringed, group):
            for distance in distances:
                for i, hop in enumerate(hops):
                    if abs(hop) == distance:
                        a_from(i, g).wait_recv()

    def split_weights(p):
        high, low = halves(wt[p])
        main = pl.ds(pl.multiple_of(p * hd, hd), hd)
        tail = pl.ds(pl.multiple_of(parts * hd + p * rest, rest), rest)
        wh[main, :] = high[:hd]
        wl[main, :] = low[:hd]
        wh[tail, :] = high[hd:]
        wl[tail, :] = low[hd:]

    lane_group = lax.div(lax.broadcasted_iota(jnp.int32, (quarter // parts, hd), 1), rest)
    sub = quarter // parts

    def c0_copy(i):
        j = lax.rem(i, half)
        return remote(cpk.at[i], c0r.at[j], c0_send.at[i], c0_recv.at[j], {"kvhead": twin})

    def c1_copy(i, d):
        p = lax.rem(y + d, parts)
        j = lax.rem(i, half)
        return remote(cpk.at[i, p], c1r.at[j, d - 1], c1_send.at[j, d - 1], c1_recv.at[j, d - 1], {"kvhead": 2 * p + c})

    def c2_copy(i):
        j, slot = lax.rem(i, half), lax.rem(s, half)
        return remote(red.at[j], c2r.at[slot], c2_send.at[j], c2_recv.at[slot], {"kvhead": 2 * y + seq_half, "seq": i})

    def mine(i):
        return lax.div(i, half) == c

    def merge(slots):
        for i in slots:
            @pl.when(mine(i))
            def _():
                c0_copy(i).wait_recv()
                for p in range(parts):
                    cpk[i, p] = cpk[i, p] + c0r[lax.rem(i, half), p]
                for d in range(1, parts):
                    c1_copy(i, d).start()

    def finish(slots):
        for i in slots:
            @pl.when(mine(i))
            def _():
                j = lax.rem(i, half)
                total = cpk[i, y]
                for d in range(1, parts):
                    c1_copy(i, d).wait_recv()
                    total = total + c1r[j, d - 1]

                @pl.when(i == s)
                def _():
                    c2r[j] = total

                @pl.when(i != s)
                def _():
                    red[j] = total
                    c2_copy(i).start()

    def project(slots):
        a = jnp.concatenate(
            [jnp.concatenate([abuf[i, g] for g in range(group)], axis=1) for i in slots], axis=0
        )
        n = len(slots) * quarter
        high, low = halves(a)
        both = dot_nt(jnp.concatenate([high, low], axis=0), wh[...])
        out = both[:n] + both[n:] + dot_nt(high, wl[...])
        for m, i in enumerate(slots):
            block = out[m * quarter:(m + 1) * quarter]
            tail = block[:, parts * hd:]
            for p in range(parts):
                cpk[i, p, :quarter] = block[:, p * hd:(p + 1) * hd]
                packed = jnp.zeros((sub, hd), F32)
                for g in range(parts):
                    piece = tail[g * sub:(g + 1) * sub]
                    shift = (rest * (g - p)) % hd
                    if shift:
                        piece = pltpu.roll(piece, shift, 1)
                    packed = jnp.where(lane_group == g, piece, packed)
                cpk[i, p, quarter:] = packed

            @pl.when(jnp.logical_not(mine(i)))
            def _():
                c0_copy(i).start()


    steps = [[s]] + [[at_z(-1), at_z(1)], [at_z(-2), at_z(2)], [at_z(-3), at_z(3), at_z(4)]]
    normalize(0)
    normalize(1)
    normalize(2)
    relay(1, 0)
    normalize(3)
    relay(1, 1)
    normalize(4)
    w_takes[0].wait_recv()
    w_takes[1].wait_recv()
    w_steps[2].start()
    w_steps[3].start()
    for p in (0, -1, 1):
        split_weights(at_x(p))
    relay(2, 0)
    forward(2)
    relay(2, 1)
    forward(3)
    forward(4)
    w_takes[2].wait_recv()
    w_takes[3].wait_recv()
    split_weights(at_x(2))
    project(steps[0])
    relay(3, 0)
    arrived(1)
    project(steps[1])
    relay(3, 1)
    merge(steps[0])
    project(steps[2])
    merge(steps[1])
    merge(steps[2])
    relay(4, 0)
    relay(4, 1)
    arrived(3, 4)
    project(steps[3])
    merge(steps[3])
    finish(steps[0])
    finish(steps[1])
    finish(steps[2])
    finish(steps[3])

    for i in range(len(hops)):
        for n in range(pieces):
            kv_out(i, n).wait_send()
    for copy in w_steps:
        copy.wait_send()

    def drain(g, carry):
        for d in range(1, parts):
            rs_copy(d, g).wait_send()
            den_copy(d, g).wait_send()
        return carry

    lax.fori_loop(0, group, drain, 0)
    for g in range(group):
        if g < ringed:
            for t in range(half - 1):
                a_copy(t, g, at_z(-t), right).wait_send()
                a_copy(half + t, g, at_z(t), left).wait_send()
            a_last(g).wait_send()
        else:
            for i in range(len(hops)):
                a_out(i, g).wait_send()

    def drain_c(i, carry):
        @pl.when(mine(i))
        def _():
            for d in range(1, parts):
                c1_copy(i, d).wait_send()

        @pl.when(jnp.logical_not(mine(i)))
        def _():
            c0_copy(i).wait_send()

        return carry

    lax.fori_loop(0, count, drain_c, 0)

    def arrive(j, carry):
        @pl.when(half * c + j != s)
        def _():
            remote(red.at[j], c2r.at[j], c2_send.at[j], c2_recv.at[j], {"kvhead": twin}).wait_recv()
            c2_copy(half * c + j).wait_send()

        return carry

    lax.fori_loop(0, half, arrive, 0)

    lane = lax.broadcasted_iota(jnp.int32, (quarter, hd), 1)
    for tile in range(parts + 1):
        value = None
        if tile < parts:
            value = c2r[tile, :quarter]
            if tile:
                value = pltpu.roll(value, rest * tile, 1)
        if tile > 0:
            j = tile - 1
            before = c2r[j, :quarter]
            if j:
                before = pltpu.roll(before, rest * j, 1)
            packed = c2r[j, quarter:]
            tail = jnp.concatenate(
                [pltpu.roll(packed, (rest * (j - g)) % hd, 1) if (j - g) % parts else packed for g in range(parts)], axis=0
            )
            value = tail if value is None else jnp.where(lane < rest * tile, tail, value)
            if j:
                value = jnp.where(lane < rest * j, before, value)
        o_ref[:, tile * hd:(tile + 1) * hd] = value


def local(queries, keys, values, w_out, *, parts, count):
    rows, group, hd = queries.shape
    quarter = rows // parts
    depth, wide = w_out.shape
    half = count // 2
    packed = quarter * wide // hd
    columns = parts * wide
    keys_all = count * quarter
    dma = pltpu.SemaphoreType.DMA
    any_space = pl.BlockSpec(memory_space=pl.ANY)
    return pl.pallas_call(
        kernel,
        out_shape=pltpu.VMEM((quarter, half * wide), F32),
        in_specs=[any_space] * 4,
        out_specs=pl.BlockSpec(memory_space=pltpu.VMEM),
        scratch_shapes=[
            pltpu.VMEM((group, rows, hd), F32),
            pltpu.VMEM((count, 2, quarter, hd), F32),
            pltpu.VMEM((parts, wide, depth), F32),
            pltpu.VMEM((group, rows, 2 * hd), BF16),
            pltpu.VMEM((keys_all, 2 * hd), BF16),
            pltpu.VMEM((keys_all, hd), BF16),
            pltpu.VMEM((keys_all, 2 * hd), BF16),
            pltpu.VMEM((group, parts, quarter, hd), F32),
            pltpu.VMEM((parts - 1, group, quarter, hd), F32),
            pltpu.VMEM((group, parts, 1, hd), F32),
            pltpu.VMEM((parts - 1, group, 1, hd), F32),
            pltpu.VMEM((count, group, quarter, hd), F32),
            pltpu.VMEM((columns, depth), BF16),
            pltpu.VMEM((columns, depth), BF16),
            pltpu.VMEM((count, parts, packed, hd), F32),
            pltpu.VMEM((half, parts, packed, hd), F32),
            pltpu.VMEM((half, parts - 1, packed, hd), F32),
            pltpu.VMEM((half, packed, hd), F32),
            pltpu.VMEM((half, packed, hd), F32),
            dma((4,)),
            dma((count - 1, 4)),
            dma((count - 1, 4)),
            dma((4,)),
            dma((4,)),
            dma((parts - 1, group)),
            dma((parts - 1, group)),
            dma((parts - 1, group)),
            dma((parts - 1, group)),
            dma((count - 1, group)),
            dma((count - 1, group)),
            dma((count,)),
            dma((half,)),
            dma((half, parts - 1)),
            dma((half, parts - 1)),
            dma((half,)),
            dma((half,)),
        ],
        compiler_params=pltpu.CompilerParams(
            collective_id=0, has_side_effects=True, vmem_limit_bytes=60 * 1024 * 1024
        ),
        name="power_attention",
    )(
        jnp.transpose(queries, (1, 0, 2)),
        keys.reshape(rows, hd),
        values.reshape(rows, hd),
        w_out.T,
    )


def solution(mesh):
    body = functools.partial(
        local, parts=mesh.shape["feature"], count=mesh.shape["seq"]
    )
    in_specs = (
        P("seq", "kvhead", None),
        P("seq", "kvhead", None),
        P("seq", "kvhead", None),
        P("kvhead", ("feature", "seq")),
    )
    out_specs = P(("seq", "feature"), "kvhead")
    return jax.shard_map(body, mesh=mesh, in_specs=in_specs, out_specs=out_specs, check_vma=False)
```

```python
import functools

import jax
import jax.numpy as jnp
from jax import lax
from jax.experimental import pallas as pl
from jax.experimental.pallas import tpu as pltpu
from jax.sharding import PartitionSpec as P

MESH = pl.DeviceIdType.MESH
NT = (((1,), (1,)), ((), ()))
F32 = jnp.float32
BF16 = jnp.bfloat16


def halves(x):
    high = x.astype(BF16)
    return high, (x - high.astype(F32)).astype(BF16)


def dot(a, b):
    return jnp.dot(a, b, preferred_element_type=F32)


def dot_nt(a, b):
    return lax.dot_general(a, b, NT, preferred_element_type=F32)


def kernel(
    q_hbm, k_hbm, v_hbm, w_hbm, o_ref,
    qv, kv, wt, qcat, kcat, klow, vcat, rs_src, rs_rcv, den_src, den_rcv, abuf, wh, wl, cpk, c0r, c1r, red, c2r,
    load_sem, kv_send, kv_recv, w_send, w_recv, rs_send, rs_recv, den_send, den_recv, a_send, a_recv,
    c0_send, c0_recv, c1_send, c1_recv, c2_send, c2_recv,
    line_known, side_known, cross_known,
):
    group, rows, hd = q_hbm.shape
    parts = wt.shape[0]
    count = kv.shape[0]
    heads = 2 * parts
    quarter = rows // parts
    half = count // 2
    wide = w_hbm.shape[0]
    rest = wide - hd
    lanes = hd // parts
    f = lax.axis_index("feature")
    k = lax.axis_index("kvhead")
    s = lax.axis_index("seq")
    y, c = lax.div(k, 2), lax.rem(k, 2)
    twin = k + 1 - 2 * c
    seq_half = lax.div(s, half)

    def at_z(d):
        return lax.rem(s + d + count, count)

    def at_x(d):
        return lax.rem(f + d + parts, parts)

    right, left = at_z(1), at_z(-1)

    own = pl.ds(pl.multiple_of(f * quarter, quarter), quarter)
    loads = [
        pltpu.make_async_copy(w_hbm, wt.at[f], load_sem.at[0]),
        pltpu.make_async_copy(k_hbm.at[own], kv.at[s, 0], load_sem.at[1]),
        pltpu.make_async_copy(v_hbm.at[own], kv.at[s, 1], load_sem.at[2]),
        pltpu.make_async_copy(q_hbm, qv, load_sem.at[3]),
    ]
    for load in loads:
        load.start()

    barrier = pltpu.get_barrier_semaphore()

    def signal(semaphore, where):
        pl.semaphore_signal(semaphore, inc=1, device_id=where, device_id_type=MESH)

    beside = [{"kvhead": lax.rem(k + d, heads)} for d in (2, heads - 2)]
    second = [{"seq": at_z(d)} for d in (2, -2)]
    near = [{"feature": at_x(d)} for d in range(1, parts)] + [{"seq": right}, {"seq": left}, {"kvhead": twin}]
    near = near + beside + second
    for where in near:
        signal(barrier, where)
    loads[1].wait()
    loads[2].wait()
    pl.semaphore_wait(barrier, len(near))
    for where in second:
        signal(line_known, where)
    for where in beside:
        signal(side_known, where)

    def known():
        pl.semaphore_wait(line_known, len(second))
        pl.semaphore_wait(side_known, len(beside))
        signal(cross_known, {"kvhead": twin})

    def remote(src, dst, send, recv, where):
        return pltpu.make_async_remote_copy(
            src_ref=src, dst_ref=dst, send_sem=send, recv_sem=recv, device_id=where, device_id_type=MESH
        )

    pieces = 4
    piece = 2 * quarter // pieces
    hops = (2, -2, 1, -1, 3, -3, 4)

    def kv_copy(i, n, slot, where):
        ref = kv.at[slot, n * piece // quarter, pl.ds(n * piece % quarter, piece)]
        return remote(ref, ref, kv_send.at[i, n], kv_recv.at[i, n], {"seq": where})

    def kv_from(i, n):
        return kv_copy(i, n, at_z(-hops[i]), right)

    def kv_out(i, n):
        if i < 4:
            return kv_copy(i, n, s, at_z(hops[i]))
        if i < 6:
            step = 2 if i == 4 else -2
            return kv_copy(i, n, at_z(-step), at_z(step // 2))
        step = 2 if n < pieces // 2 else -2
        return kv_copy(i, n, at_z(-step), at_z(step))

    def kv_take(slot):
        place = pl.ds(pl.multiple_of(slot * quarter, quarter), quarter)
        kh, kl = halves(kv[slot, 0])
        vh, vl = halves(kv[slot, 1])
        kcat[place, :hd] = kh
        kcat[place, hd:] = kh
        klow[place, :] = kl
        vcat[place, :hd] = vh
        vcat[place, hd:] = vl

    for i in range(4):
        for n in range(pieces):
            kv_out(i, n).start()

    def w_copy(i, src, where):
        return remote(src, src, w_send.at[i], w_recv.at[i], {"feature": where})

    w_top, w_low = pl.ds(0, wide // 2), pl.ds(wide // 2, wide // 2)
    w_steps = [
        w_copy(0, wt.at[f], at_x(1)),
        w_copy(1, wt.at[f], at_x(-1)),
        w_copy(2, wt.at[at_x(-1), w_top], at_x(1)),
        w_copy(3, wt.at[at_x(1), w_low], at_x(-1)),
    ]
    w_takes = [
        w_copy(0, wt.at[at_x(-1)], at_x(1)),
        w_copy(1, wt.at[at_x(1)], at_x(-1)),
        w_copy(2, wt.at[at_x(2), w_top], at_x(1)),
        w_copy(3, wt.at[at_x(2), w_low], at_x(-1)),
    ]
    loads[0].wait()
    w_steps[0].start()
    w_steps[1].start()

    loads[3].wait()
    for g in range(group):
        qh, ql = halves(qv[g] * (hd ** -0.5))
        qcat[g, :, :hd] = qh
        qcat[g, :, hd:] = ql
    kv_take(s)
    for n in range(pieces):
        kv_from(0, n).wait_recv()
        kv_out(4, n).start()
        if n < pieces // 2:
            kv_out(6, n).start()
        kv_from(1, n).wait_recv()
        kv_out(5, n).start()
        if n >= pieces // 2:
            kv_out(6, n).start()
    kv_take(at_z(-2))
    kv_take(at_z(2))
    for i in range(2, len(hops)):
        for n in range(pieces):
            kv_from(i, n).wait_recv()
        kv_take(at_z(-hops[i]))

    def rs_copy(d, g):
        to = at_x(d)
        return remote(rs_src.at[g, to], rs_rcv.at[d - 1, g], rs_send.at[d - 1, g], rs_recv.at[d - 1, g], {"feature": to})

    def den_copy(d, g):
        to = at_x(d)
        return remote(
            den_src.at[g, to], den_rcv.at[d - 1, g], den_send.at[d - 1, g], den_recv.at[d - 1, g], {"feature": to}
        )

    shape = (rows, count * quarter)
    column = lax.broadcasted_iota(jnp.int32, shape, 1)
    key_pos = lax.shift_right_logical(column, 6) * rows + f * quarter + jnp.bitwise_and(column, quarter - 1)
    query_pos = s * rows + lax.broadcasted_iota(jnp.int32, shape, 0)
    allowed = key_pos <= query_pos
    diagonal = lax.broadcasted_iota(jnp.int32, (quarter, hd), 0) == lax.broadcasted_iota(jnp.int32, (quarter, hd), 1)

    def head(g, carry):
        scores = dot_nt(qcat[g], kcat[...]) + dot_nt(qcat[g, :, :hd], klow[...])
        squared = jnp.where(allowed, scores * scores, 0.0)
        ph, plow = halves(squared)
        both = dot(ph, vcat[...])
        numerator = both[:, :hd] + both[:, hd:] + dot(plow, vcat[:, :hd])
        denominator = jnp.sum(squared, axis=1, keepdims=True)
        for p in range(parts):
            part = slice(p * quarter, (p + 1) * quarter)
            rs_src[g, p] = numerator[part]
            spread = jnp.where(diagonal, jnp.broadcast_to(denominator[part], (quarter, hd)), 0.0)
            den_src[g, p] = jnp.sum(spread, axis=0, keepdims=True)
        for d in range(1, parts):
            den_copy(d, g).start()
            rs_copy(d, g).start()
        return carry

    lax.fori_loop(0, group, head, 0)

    def a_copy(i, g, slot, where):
        return remote(abuf.at[slot, g], abuf.at[slot, g], a_send.at[i, g], a_recv.at[i, g], {"seq": where})

    ringed = 2

    def normalize(g):
        for d in range(1, parts):
            den_copy(d, g).wait_recv()
            rs_copy(d, g).wait_recv()
        total = rs_src[g, f] + rs_rcv[0, g]
        line = den_src[g, f] + den_rcv[0, g]
        for d in range(1, parts - 1):
            total = total + rs_rcv[d, g]
            line = line + den_rcv[d, g]
        line = jnp.broadcast_to(line, (quarter, hd))
        denominator = jnp.sum(jnp.where(diagonal, line, 0.0), axis=1, keepdims=True)
        abuf[s, g] = total / (denominator + 1.0)
        if g < ringed:
            a_copy(0, g, s, right).start()
            a_copy(half, g, s, left).start()
        else:
            for i in range(4):
                a_out(i, g).start()

    def a_last(g):
        if g % 2 == 0:
            return a_copy(half - 1, g, at_z(1 - half), right)
        return a_copy(half - 1, g, at_z(half - 1), left)

    def relay(t, g):
        a_copy(t - 1, g, at_z(-t), right).wait_recv()
        if t < half:
            a_copy(half + t - 1, g, at_z(t), left).wait_recv()
        if t < half - 1:
            a_copy(t, g, at_z(-t), right).start()
            a_copy(half + t, g, at_z(t), left).start()
        if t == half - 1:
            a_last(g).start()

    def a_from(i, g):
        return a_copy(i, g, at_z(-hops[i]), right)

    def a_out(i, g):
        if i < 4:
            return a_copy(i, g, s, at_z(hops[i]))
        if i < 6:
            step = 2 if i == 4 else -2
            return a_copy(i, g, at_z(-step), at_z(step // 2))
        step = 2 if g % 2 == 0 else -2
        return a_copy(i, g, at_z(-step), at_z(step))

    def forward(g):
        a_from(0, g).wait_recv()
        if g % 2 == 0:
            a_out(6, g).start()
        a_out(4, g).start()
        a_from(1, g).wait_recv()
        if g % 2 == 1:
            a_out(6, g).start()
        a_out(5, g).start()

    def arrived(*distances):
        for g in range(ringed, group):
            for distance in distances:
                for i, hop in enumerate(hops):
                    if abs(hop) == distance:
                        a_from(i, g).wait_recv()

    def split_weights(p):
        high, low = halves(wt[p])
        main = pl.ds(pl.multiple_of(p * hd, hd), hd)
        tail = pl.ds(pl.multiple_of(parts * hd + p * rest, rest), rest)
        wh[main, :] = high[:hd]
        wl[main, :] = low[:hd]
        wh[tail, :] = high[hd:]
        wl[tail, :] = low[hd:]

    lane_group = lax.div(lax.broadcasted_iota(jnp.int32, (quarter // parts, hd), 1), rest)
    sub = quarter // parts

    def c0_copy(i):
        j = lax.rem(i, half)
        return remote(cpk.at[i], c0r.at[j], c0_send.at[i], c0_recv.at[j], {"kvhead": twin})

    def c1_copy(i, d):
        p = lax.rem(y + d, parts)
        j = lax.rem(i, half)
        return remote(cpk.at[i, p], c1r.at[j, d - 1], c1_send.at[j, d - 1], c1_recv.at[j, d - 1], {"kvhead": 2 * p + c})

    def c2_copy(i):
        j, slot = lax.rem(i, half), lax.rem(s, half)
        return remote(red.at[j], c2r.at[slot], c2_send.at[j], c2_recv.at[slot], {"kvhead": 2 * y + seq_half, "seq": i})

    def mine(i):
        return lax.div(i, half) == c

    def merge(slots):
        for i in slots:
            @pl.when(mine(i))
            def _():
                c0_copy(i).wait_recv()
                for p in range(parts):
                    cpk[i, p] = cpk[i, p] + c0r[lax.rem(i, half), p]
                for d in range(1, parts):
                    c1_copy(i, d).start()

    def finish(slots):
        for i in slots:
            @pl.when(mine(i))
            def _():
                j = lax.rem(i, half)
                total = cpk[i, y]
                for d in range(1, parts):
                    c1_copy(i, d).wait_recv()
                    total = total + c1r[j, d - 1]

                @pl.when(i == s)
                def _():
                    c2r[j] = total

                @pl.when(i != s)
                def _():
                    red[j] = total
                    c2_copy(i).start()

    def project(slots):
        a = jnp.concatenate(
            [jnp.concatenate([abuf[i, g] for g in range(group)], axis=1) for i in slots], axis=0
        )
        n = len(slots) * quarter
        high, low = halves(a)
        both = dot_nt(jnp.concatenate([high, low], axis=0), wh[...])
        out = both[:n] + both[n:] + dot_nt(high, wl[...])
        for m, i in enumerate(slots):
            block = out[m * quarter:(m + 1) * quarter]
            tail = block[:, parts * hd:]
            for p in range(parts):
                cpk[i, p, :quarter] = block[:, p * hd:(p + 1) * hd]
                packed = jnp.zeros((sub, hd), F32)
                for g in range(parts):
                    piece = tail[g * sub:(g + 1) * sub]
                    shift = (rest * (g - p)) % hd
                    if shift:
                        piece = pltpu.roll(piece, shift, 1)
                    packed = jnp.where(lane_group == g, piece, packed)
                cpk[i, p, quarter:] = packed

            @pl.when(jnp.logical_not(mine(i)))
            def _():
                c0_copy(i).start()


    steps = [[s]] + [[at_z(-1), at_z(1)], [at_z(-2), at_z(2)], [at_z(-3), at_z(3), at_z(4)]]
    normalize(0)
    normalize(1)
    normalize(2)
    relay(1, 0)
    normalize(3)
    relay(1, 1)
    normalize(4)
    w_takes[0].wait_recv()
    w_takes[1].wait_recv()
    w_steps[2].start()
    w_steps[3].start()
    for p in (0, -1, 1):
        split_weights(at_x(p))
    relay(2, 0)
    forward(2)
    relay(2, 1)
    forward(3)
    known()
    forward(4)
    w_takes[2].wait_recv()
    w_takes[3].wait_recv()
    split_weights(at_x(2))
    project(steps[0])
    relay(3, 0)
    arrived(1)
    project(steps[1])
    relay(3, 1)
    merge(steps[0])
    project(steps[2])
    merge(steps[1])
    merge(steps[2])
    relay(4, 0)
    relay(4, 1)
    arrived(3, 4)
    project(steps[3])
    merge(steps[3])
    pl.semaphore_wait(cross_known, 1)
    finish(steps[0])
    finish(steps[1])
    finish(steps[2])
    finish(steps[3])

    for i in range(len(hops)):
        for n in range(pieces):
            kv_out(i, n).wait_send()
    for copy in w_steps:
        copy.wait_send()

    def drain(g, carry):
        for d in range(1, parts):
            rs_copy(d, g).wait_send()
            den_copy(d, g).wait_send()
        return carry

    lax.fori_loop(0, group, drain, 0)
    for g in range(group):
        if g < ringed:
            for t in range(half - 1):
                a_copy(t, g, at_z(-t), right).wait_send()
                a_copy(half + t, g, at_z(t), left).wait_send()
            a_last(g).wait_send()
        else:
            for i in range(len(hops)):
                a_out(i, g).wait_send()

    def drain_c(i, carry):
        @pl.when(mine(i))
        def _():
            for d in range(1, parts):
                c1_copy(i, d).wait_send()

        @pl.when(jnp.logical_not(mine(i)))
        def _():
            c0_copy(i).wait_send()

        return carry

    lax.fori_loop(0, count, drain_c, 0)

    def arrive(j, carry):
        @pl.when(half * c + j != s)
        def _():
            remote(red.at[j], c2r.at[j], c2_send.at[j], c2_recv.at[j], {"kvhead": twin}).wait_recv()
            c2_copy(half * c + j).wait_send()

        return carry

    lax.fori_loop(0, half, arrive, 0)

    lane = lax.broadcasted_iota(jnp.int32, (quarter, hd), 1)
    for tile in range(parts + 1):
        value = None
        if tile < parts:
            value = c2r[tile, :quarter]
            if tile:
                value = pltpu.roll(value, rest * tile, 1)
        if tile > 0:
            j = tile - 1
            before = c2r[j, :quarter]
            if j:
                before = pltpu.roll(before, rest * j, 1)
            packed = c2r[j, quarter:]
            tail = jnp.concatenate(
                [pltpu.roll(packed, (rest * (j - g)) % hd, 1) if (j - g) % parts else packed for g in range(parts)], axis=0
            )
            value = tail if value is None else jnp.where(lane < rest * tile, tail, value)
            if j:
                value = jnp.where(lane < rest * j, before, value)
        o_ref[:, tile * hd:(tile + 1) * hd] = value


def local(queries, keys, values, w_out, *, parts, count):
    rows, group, hd = queries.shape
    quarter = rows // parts
    depth, wide = w_out.shape
    half = count // 2
    packed = quarter * wide // hd
    columns = parts * wide
    keys_all = count * quarter
    dma = pltpu.SemaphoreType.DMA
    any_space = pl.BlockSpec(memory_space=pl.ANY)
    return pl.pallas_call(
        kernel,
        out_shape=pltpu.VMEM((quarter, half * wide), F32),
        in_specs=[any_space] * 4,
        out_specs=pl.BlockSpec(memory_space=pltpu.VMEM),
        scratch_shapes=[
            pltpu.VMEM((group, rows, hd), F32),
            pltpu.VMEM((count, 2, quarter, hd), F32),
            pltpu.VMEM((parts, wide, depth), F32),
            pltpu.VMEM((group, rows, 2 * hd), BF16),
            pltpu.VMEM((keys_all, 2 * hd), BF16),
            pltpu.VMEM((keys_all, hd), BF16),
            pltpu.VMEM((keys_all, 2 * hd), BF16),
            pltpu.VMEM((group, parts, quarter, hd), F32),
            pltpu.VMEM((parts - 1, group, quarter, hd), F32),
            pltpu.VMEM((group, parts, 1, hd), F32),
            pltpu.VMEM((parts - 1, group, 1, hd), F32),
            pltpu.VMEM((count, group, quarter, hd), F32),
            pltpu.VMEM((columns, depth), BF16),
            pltpu.VMEM((columns, depth), BF16),
            pltpu.VMEM((count, parts, packed, hd), F32),
            pltpu.VMEM((half, parts, packed, hd), F32),
            pltpu.VMEM((half, parts - 1, packed, hd), F32),
            pltpu.VMEM((half, packed, hd), F32),
            pltpu.VMEM((half, packed, hd), F32),
            dma((4,)),
            dma((count - 1, 4)),
            dma((count - 1, 4)),
            dma((4,)),
            dma((4,)),
            dma((parts - 1, group)),
            dma((parts - 1, group)),
            dma((parts - 1, group)),
            dma((parts - 1, group)),
            dma((count - 1, group)),
            dma((count - 1, group)),
            dma((count,)),
            dma((half,)),
            dma((half, parts - 1)),
            dma((half, parts - 1)),
            dma((half,)),
            dma((half,)),
            pltpu.SemaphoreType.REGULAR,
            pltpu.SemaphoreType.REGULAR,
            pltpu.SemaphoreType.REGULAR,
        ],
        compiler_params=pltpu.CompilerParams(
            collective_id=0, has_side_effects=True, vmem_limit_bytes=60 * 1024 * 1024
        ),
        name="power_attention",
    )(
        jnp.transpose(queries, (1, 0, 2)),
        keys.reshape(rows, hd),
        values.reshape(rows, hd),
        w_out.T,
    )


def solution(mesh):
    body = functools.partial(
        local, parts=mesh.shape["feature"], count=mesh.shape["seq"]
    )
    in_specs = (
        P("seq", "kvhead", None),
        P("seq", "kvhead", None),
        P("seq", "kvhead", None),
        P("kvhead", ("feature", "seq")),
    )
    out_specs = P(("seq", "feature"), "kvhead")
    return jax.shard_map(body, mesh=mesh, in_specs=in_specs, out_specs=out_specs, check_vma=False)
```

```python
import functools

import jax
import jax.numpy as jnp
from jax import lax
from jax.experimental import pallas as pl
from jax.experimental.pallas import tpu as pltpu
from jax.sharding import PartitionSpec as P

MESH = pl.DeviceIdType.MESH
NT = (((1,), (1,)), ((), ()))
F32 = jnp.float32
BF16 = jnp.bfloat16


def halves(x):
    high = x.astype(BF16)
    return high, (x - high.astype(F32)).astype(BF16)


def dot(a, b):
    return jnp.dot(a, b, preferred_element_type=F32)


def dot_nt(a, b):
    return lax.dot_general(a, b, NT, preferred_element_type=F32)


def kernel(
    q_hbm, k_hbm, v_hbm, w_hbm, o_ref,
    qv, kv, wt, qcat, kcat, klow, vcat, rs_src, rs_rcv, den_src, den_rcv, abuf, wh, wl, cpk, c0r, c1r, red, c2r,
    load_sem, kv_send, kv_recv, w_send, w_recv, rs_send, rs_recv, den_send, den_recv, a_send, a_recv,
    c0_send, c0_recv, c1_send, c1_recv, c2_send, c2_recv,
    line_known, side_known, cross_known,
):
    group, rows, hd = q_hbm.shape
    parts = wt.shape[0]
    count = kv.shape[0]
    heads = 2 * parts
    quarter = rows // parts
    half = count // 2
    wide = w_hbm.shape[0]
    rest = wide - hd
    lanes = hd // parts
    f = lax.axis_index("feature")
    k = lax.axis_index("kvhead")
    s = lax.axis_index("seq")
    y, c = lax.div(k, 2), lax.rem(k, 2)
    twin = k + 1 - 2 * c
    seq_half = lax.div(s, half)

    def at_z(d):
        return lax.rem(s + d + count, count)

    def at_x(d):
        return lax.rem(f + d + parts, parts)

    right, left = at_z(1), at_z(-1)

    own = pl.ds(pl.multiple_of(f * quarter, quarter), quarter)
    loads = [
        pltpu.make_async_copy(w_hbm, wt.at[f], load_sem.at[0]),
        pltpu.make_async_copy(k_hbm.at[own], kv.at[s, 0], load_sem.at[1]),
        pltpu.make_async_copy(v_hbm.at[own], kv.at[s, 1], load_sem.at[2]),
        pltpu.make_async_copy(q_hbm, qv, load_sem.at[3]),
    ]
    for load in loads:
        load.start()

    barrier = pltpu.get_barrier_semaphore()

    def signal(semaphore, where):
        pl.semaphore_signal(semaphore, inc=1, device_id=where, device_id_type=MESH)

    beside = [{"kvhead": lax.rem(k + d, heads)} for d in (2, heads - 2)]
    second = [{"seq": at_z(d)} for d in (2, -2)]
    near = [{"feature": at_x(d)} for d in range(1, parts)] + [{"seq": right}, {"seq": left}, {"kvhead": twin}]
    near = near + beside + second
    for where in near:
        signal(barrier, where)
    loads[1].wait()
    loads[2].wait()
    pl.semaphore_wait(barrier, len(near))
    for where in second:
        signal(line_known, where)
    for where in beside:
        signal(side_known, where)

    def known():
        pl.semaphore_wait(line_known, len(second))
        pl.semaphore_wait(side_known, len(beside))
        signal(cross_known, {"kvhead": twin})

    def remote(src, dst, send, recv, where):
        return pltpu.make_async_remote_copy(
            src_ref=src, dst_ref=dst, send_sem=send, recv_sem=recv, device_id=where, device_id_type=MESH
        )

    pieces = 4
    piece = 2 * quarter // pieces
    hops = (2, -2, 1, -1, 3, -3, 4)

    def kv_copy(i, n, slot, where):
        ref = kv.at[slot, n * piece // quarter, pl.ds(n * piece % quarter, piece)]
        return remote(ref, ref, kv_send.at[i, n], kv_recv.at[i, n], {"seq": where})

    def kv_from(i, n):
        return kv_copy(i, n, at_z(-hops[i]), right)

    def kv_out(i, n):
        if i < 4:
            return kv_copy(i, n, s, at_z(hops[i]))
        if i < 6:
            step = 2 if i == 4 else -2
            return kv_copy(i, n, at_z(-step), at_z(step // 2))
        step = 2 if n < pieces // 2 else -2
        return kv_copy(i, n, at_z(-step), at_z(step))

    def kv_take(slot):
        place = pl.ds(pl.multiple_of(slot * quarter, quarter), quarter)
        kh, kl = halves(kv[slot, 0])
        vh, vl = halves(kv[slot, 1])
        kcat[place, :hd] = kh
        kcat[place, hd:] = kh
        klow[place, :] = kl
        vcat[place, :hd] = vh
        vcat[place, hd:] = vl

    for i in range(4):
        for n in range(pieces):
            kv_out(i, n).start()

    def w_copy(i, src, where):
        return remote(src, src, w_send.at[i], w_recv.at[i], {"feature": where})

    w_top, w_low = pl.ds(0, wide // 2), pl.ds(wide // 2, wide // 2)
    w_steps = [
        w_copy(0, wt.at[f], at_x(1)),
        w_copy(1, wt.at[f], at_x(-1)),
        w_copy(2, wt.at[at_x(-1), w_top], at_x(1)),
        w_copy(3, wt.at[at_x(1), w_low], at_x(-1)),
    ]
    w_takes = [
        w_copy(0, wt.at[at_x(-1)], at_x(1)),
        w_copy(1, wt.at[at_x(1)], at_x(-1)),
        w_copy(2, wt.at[at_x(2), w_top], at_x(1)),
        w_copy(3, wt.at[at_x(2), w_low], at_x(-1)),
    ]
    loads[0].wait()
    lead = 1
    early = s < lead

    def w_begin():
        w_steps[0].start()
        w_steps[1].start()

    pl.when(jnp.logical_not(early))(w_begin)

    loads[3].wait()
    for g in range(group):
        qh, ql = halves(qv[g] * (hd ** -0.5))
        qcat[g, :, :hd] = qh
        qcat[g, :, hd:] = ql
    kcat[...] = jnp.zeros_like(kcat)
    klow[...] = jnp.zeros_like(klow)
    vcat[...] = jnp.zeros_like(vcat)
    kv_take(s)
    def kv_second():
        for n in range(pieces):
            kv_from(0, n).wait_recv()
            kv_out(4, n).start()
            if n < pieces // 2:
                kv_out(6, n).start()
            kv_from(1, n).wait_recv()
            kv_out(5, n).start()
            if n >= pieces // 2:
                kv_out(6, n).start()

    @pl.when(s > 0)
    def _():
        kv_second()
        kv_take(at_z(-2))
        kv_take(at_z(2))

    for i in range(2, len(hops)):
        @pl.when(at_z(-hops[i]) < s)
        def _():
            for n in range(pieces):
                kv_from(i, n).wait_recv()
            kv_take(at_z(-hops[i]))


    def rs_copy(d, g):
        to = at_x(d)
        return remote(rs_src.at[g, to], rs_rcv.at[d - 1, g], rs_send.at[d - 1, g], rs_recv.at[d - 1, g], {"feature": to})

    def den_copy(d, g):
        to = at_x(d)
        return remote(
            den_src.at[g, to], den_rcv.at[d - 1, g], den_send.at[d - 1, g], den_recv.at[d - 1, g], {"feature": to}
        )

    shape = (rows, count * quarter)
    column = lax.broadcasted_iota(jnp.int32, shape, 1)
    key_pos = lax.shift_right_logical(column, 6) * rows + f * quarter + jnp.bitwise_and(column, quarter - 1)
    query_pos = s * rows + lax.broadcasted_iota(jnp.int32, shape, 0)
    allowed = key_pos <= query_pos
    diagonal = lax.broadcasted_iota(jnp.int32, (quarter, hd), 0) == lax.broadcasted_iota(jnp.int32, (quarter, hd), 1)

    def head(g, carry):
        scores = dot_nt(qcat[g], kcat[...]) + dot_nt(qcat[g, :, :hd], klow[...])
        squared = jnp.where(allowed, scores * scores, 0.0)
        ph, plow = halves(squared)
        both = dot(ph, vcat[...])
        numerator = both[:, :hd] + both[:, hd:] + dot(plow, vcat[:, :hd])
        denominator = jnp.sum(squared, axis=1, keepdims=True)
        for p in range(parts):
            part = slice(p * quarter, (p + 1) * quarter)
            rs_src[g, p] = numerator[part]
            spread = jnp.where(diagonal, jnp.broadcast_to(denominator[part], (quarter, hd)), 0.0)
            den_src[g, p] = jnp.sum(spread, axis=0, keepdims=True)
        for d in range(1, parts):
            den_copy(d, g).start()
            rs_copy(d, g).start()
        return carry

    lax.fori_loop(0, group, head, 0)

    @pl.when(s == 0)
    def _():
        kv_second()

    pl.when(early)(w_begin)

    def a_copy(i, g, slot, where):
        return remote(abuf.at[slot, g], abuf.at[slot, g], a_send.at[i, g], a_recv.at[slot, g], {"seq": where})

    def a_wait(slot, g):
        a_copy(0, g, slot, right).wait_recv()

    ringed = 2

    def normalize(g):
        for d in range(1, parts):
            den_copy(d, g).wait_recv()
            rs_copy(d, g).wait_recv()
        total = rs_src[g, f] + rs_rcv[0, g]
        line = den_src[g, f] + den_rcv[0, g]
        for d in range(1, parts - 1):
            total = total + rs_rcv[d, g]
            line = line + den_rcv[d, g]
        line = jnp.broadcast_to(line, (quarter, hd))
        denominator = jnp.sum(jnp.where(diagonal, line, 0.0), axis=1, keepdims=True)
        abuf[s, g] = total / (denominator + 1.0)
        if g < ringed:
            @pl.when(early)
            def _():
                for i in range(4):
                    a_out(i, g).start()

            @pl.when(jnp.logical_not(early))
            def _():
                r_out(0, g).start()
                r_out(4, g).start()

        else:
            for i in range(4):
                a_out(i, g).start()

    def r_out(i, g):
        if i == 3:
            step = 2 if g % 2 == 0 else -2
            return a_copy(7 + i, g, at_z(-step), at_z(step))
        if i < 3:
            return a_copy(7 + i, g, at_z(-i), right)
        return a_copy(7 + i, g, at_z(i - 4), left)

    def relay_acts(t, g):
        for slot, i, parity in ((at_z(-t), t, 0), (at_z(t), 4 + t, 1)):
            yield slot, [i, 3] if t == 2 and g % 2 == parity else [i]

    def relay(t, g):
        for slot, acts in relay_acts(t, g):
            @pl.when(slot >= lead)
            def _():
                a_wait(slot, g)
                for i in acts:
                    r_out(i, g).start()

    def a_out(i, g):
        if i < 4:
            return a_copy(i, g, s, at_z(hops[i]))
        if i < 6:
            step = 2 if i == 4 else -2
            return a_copy(i, g, at_z(-step), at_z(step // 2))
        step = 2 if g % 2 == 0 else -2
        return a_copy(i, g, at_z(-step), at_z(step))

    def pass_acts(g):
        for slot, i, parity in ((at_z(-2), 4, 0), (at_z(2), 5, 1)):
            yield slot, [6, i] if g % 2 == parity else [i]

    def pass_on(g, which):
        for slot, acts in pass_acts(g):
            @pl.when(which(slot))
            def _():
                a_wait(slot, g)
                for i in acts:
                    a_out(i, g).start()

    def first(g):
        pass_on(g, lambda slot: slot < lead)

    def forward(g):
        pass_on(g, lambda slot: slot >= lead)

    def arrived(slots):
        for slot in slots:
            away = lax.rem(s - slot + count, count)
            one = (away == 1) | (away == count - 1)
            far = (away > 2) & (away < count - 2)

            @pl.when(far | (one & (slot < lead)))
            def _():
                for g in range(ringed):
                    a_wait(slot, g)

            @pl.when(far | one)
            def _():
                for g in range(ringed, group):
                    a_wait(slot, g)

    def split_weights(p):
        high, low = halves(wt[p])
        main = pl.ds(pl.multiple_of(p * hd, hd), hd)
        tail = pl.ds(pl.multiple_of(parts * hd + p * rest, rest), rest)
        wh[main, :] = high[:hd]
        wl[main, :] = low[:hd]
        wh[tail, :] = high[hd:]
        wl[tail, :] = low[hd:]

    lane_group = lax.div(lax.broadcasted_iota(jnp.int32, (quarter // parts, hd), 1), rest)
    sub = quarter // parts

    def c0_copy(i):
        j = lax.rem(i, half)
        return remote(cpk.at[i], c0r.at[j], c0_send.at[i], c0_recv.at[j], {"kvhead": twin})

    def c1_copy(i, d):
        p = lax.rem(y + d, parts)
        j = lax.rem(i, half)
        return remote(cpk.at[i, p], c1r.at[j, d - 1], c1_send.at[j, d - 1], c1_recv.at[j, d - 1], {"kvhead": 2 * p + c})

    def c2_copy(i):
        j, slot = lax.rem(i, half), lax.rem(s, half)
        return remote(red.at[j], c2r.at[slot], c2_send.at[j], c2_recv.at[slot], {"kvhead": 2 * y + seq_half, "seq": i})

    def mine(i):
        return lax.div(i, half) == c

    def merge(slots):
        for i in slots:
            @pl.when(mine(i))
            def _():
                c0_copy(i).wait_recv()
                for p in range(parts):
                    cpk[i, p] = cpk[i, p] + c0r[lax.rem(i, half), p]
                for d in range(1, parts):
                    c1_copy(i, d).start()

    def finish(slots):
        for i in slots:
            @pl.when(mine(i))
            def _():
                j = lax.rem(i, half)
                total = cpk[i, y]
                for d in range(1, parts):
                    c1_copy(i, d).wait_recv()
                    total = total + c1r[j, d - 1]

                @pl.when(i == s)
                def _():
                    c2r[j] = total

                @pl.when(i != s)
                def _():
                    red[j] = total
                    c2_copy(i).start()

    def project(slots):
        a = jnp.concatenate(
            [jnp.concatenate([abuf[i, g] for g in range(group)], axis=1) for i in slots], axis=0
        )
        n = len(slots) * quarter
        high, low = halves(a)
        both = dot_nt(jnp.concatenate([high, low], axis=0), wh[...])
        out = both[:n] + both[n:] + dot_nt(high, wl[...])
        for m, i in enumerate(slots):
            block = out[m * quarter:(m + 1) * quarter]
            tail = block[:, parts * hd:]
            for p in range(parts):
                cpk[i, p, :quarter] = block[:, p * hd:(p + 1) * hd]
                packed = jnp.zeros((sub, hd), F32)
                for g in range(parts):
                    piece = tail[g * sub:(g + 1) * sub]
                    shift = (rest * (g - p)) % hd
                    if shift:
                        piece = pltpu.roll(piece, shift, 1)
                    packed = jnp.where(lane_group == g, piece, packed)
                cpk[i, p, quarter:] = packed

            @pl.when(jnp.logical_not(mine(i)))
            def _():
                c0_copy(i).start()


    def in_turn(place):
        chosen = jnp.int32(0)
        for here in range(count):
            def away(i):
                steps = min((here - i) % count, (i - here) % count)
                return 0.5 if i == 0 and steps > 2 else steps

            chosen = jnp.where(s == here, sorted(range(count), key=away)[place], chosen)
        return chosen

    steps = [[in_turn(n), in_turn(n + 1)] for n in range(0, count, 2)]
    first(0)
    first(1)
    first(2)
    normalize(0)
    first(3)
    normalize(1)
    first(4)
    normalize(2)
    pl.when(early)(lambda: normalize(3))
    pl.when(early)(lambda: normalize(4))
    relay(1, 0)
    pl.when(jnp.logical_not(early))(lambda: normalize(3))
    relay(1, 1)
    pl.when(jnp.logical_not(early))(lambda: normalize(4))
    w_takes[0].wait_recv()
    w_takes[1].wait_recv()
    w_steps[2].start()
    w_steps[3].start()
    for p in (0, -1, 1):
        split_weights(at_x(p))
    relay(2, 0)
    forward(2)
    relay(2, 1)
    forward(3)
    known()
    forward(4)
    w_takes[2].wait_recv()
    w_takes[3].wait_recv()
    split_weights(at_x(2))
    arrived(steps[0])
    project(steps[0])
    arrived(steps[1])
    project(steps[1])
    merge(steps[0])
    arrived(steps[2])
    project(steps[2])
    merge(steps[1])
    arrived(steps[3])
    project(steps[3])
    merge(steps[2])
    pl.semaphore_wait(cross_known, 1)
    finish(steps[0])
    merge(steps[3])
    finish(steps[1])
    finish(steps[2])
    finish(steps[3])

    for i in range(len(hops)):
        for n in range(pieces):
            kv_out(i, n).wait_send()
    for i in range(2, len(hops)):
        @pl.when(at_z(-hops[i]) > s)
        def _():
            for n in range(pieces):
                kv_from(i, n).wait_recv()

    for copy in w_steps:
        copy.wait_send()

    def drain(g, carry):
        for d in range(1, parts):
            rs_copy(d, g).wait_send()
            den_copy(d, g).wait_send()
        return carry

    lax.fori_loop(0, group, drain, 0)
    for g in range(group):
        if g < ringed:
            @pl.when(early)
            def _():
                for i in range(4):
                    a_out(i, g).wait_send()

            @pl.when(jnp.logical_not(early))
            def _():
                r_out(0, g).wait_send()
                r_out(4, g).wait_send()

            for t in (1, 2):
                for slot, acts in relay_acts(t, g):
                    @pl.when(slot >= lead)
                    def _():
                        for i in acts:
                            r_out(i, g).wait_send()

            for slot, acts in pass_acts(g):
                @pl.when(slot < lead)
                def _():
                    for i in acts:
                        a_out(i, g).wait_send()

        else:
            for i in range(len(hops)):
                a_out(i, g).wait_send()

    def drain_c(i, carry):
        @pl.when(mine(i))
        def _():
            for d in range(1, parts):
                c1_copy(i, d).wait_send()

        @pl.when(jnp.logical_not(mine(i)))
        def _():
            c0_copy(i).wait_send()

        return carry

    lax.fori_loop(0, count, drain_c, 0)

    def arrive(j, carry):
        @pl.when(half * c + j != s)
        def _():
            remote(red.at[j], c2r.at[j], c2_send.at[j], c2_recv.at[j], {"kvhead": twin}).wait_recv()
            c2_copy(half * c + j).wait_send()

        return carry

    lax.fori_loop(0, half, arrive, 0)

    lane = lax.broadcasted_iota(jnp.int32, (quarter, hd), 1)
    for tile in range(parts + 1):
        value = None
        if tile < parts:
            value = c2r[tile, :quarter]
            if tile:
                value = pltpu.roll(value, rest * tile, 1)
        if tile > 0:
            j = tile - 1
            before = c2r[j, :quarter]
            if j:
                before = pltpu.roll(before, rest * j, 1)
            packed = c2r[j, quarter:]
            tail = jnp.concatenate(
                [pltpu.roll(packed, (rest * (j - g)) % hd, 1) if (j - g) % parts else packed for g in range(parts)], axis=0
            )
            value = tail if value is None else jnp.where(lane < rest * tile, tail, value)
            if j:
                value = jnp.where(lane < rest * j, before, value)
        o_ref[:, tile * hd:(tile + 1) * hd] = value


def local(queries, keys, values, w_out, *, parts, count):
    rows, group, hd = queries.shape
    quarter = rows // parts
    depth, wide = w_out.shape
    half = count // 2
    packed = quarter * wide // hd
    columns = parts * wide
    keys_all = count * quarter
    dma = pltpu.SemaphoreType.DMA
    any_space = pl.BlockSpec(memory_space=pl.ANY)
    return pl.pallas_call(
        kernel,
        out_shape=pltpu.VMEM((quarter, half * wide), F32),
        in_specs=[any_space] * 4,
        out_specs=pl.BlockSpec(memory_space=pltpu.VMEM),
        scratch_shapes=[
            pltpu.VMEM((group, rows, hd), F32),
            pltpu.VMEM((count, 2, quarter, hd), F32),
            pltpu.VMEM((parts, wide, depth), F32),
            pltpu.VMEM((group, rows, 2 * hd), BF16),
            pltpu.VMEM((keys_all, 2 * hd), BF16),
            pltpu.VMEM((keys_all, hd), BF16),
            pltpu.VMEM((keys_all, 2 * hd), BF16),
            pltpu.VMEM((group, parts, quarter, hd), F32),
            pltpu.VMEM((parts - 1, group, quarter, hd), F32),
            pltpu.VMEM((group, parts, 1, hd), F32),
            pltpu.VMEM((parts - 1, group, 1, hd), F32),
            pltpu.VMEM((count, group, quarter, hd), F32),
            pltpu.VMEM((columns, depth), BF16),
            pltpu.VMEM((columns, depth), BF16),
            pltpu.VMEM((count, parts, packed, hd), F32),
            pltpu.VMEM((half, parts, packed, hd), F32),
            pltpu.VMEM((half, parts - 1, packed, hd), F32),
            pltpu.VMEM((half, packed, hd), F32),
            pltpu.VMEM((half, packed, hd), F32),
            dma((4,)),
            dma((count - 1, 4)),
            dma((count - 1, 4)),
            dma((4,)),
            dma((4,)),
            dma((parts - 1, group)),
            dma((parts - 1, group)),
            dma((parts - 1, group)),
            dma((parts - 1, group)),
            dma((2 * count - 2, group)),
            dma((count, group)),
            dma((count,)),
            dma((half,)),
            dma((half, parts - 1)),
            dma((half, parts - 1)),
            dma((half,)),
            dma((half,)),
            pltpu.SemaphoreType.REGULAR,
            pltpu.SemaphoreType.REGULAR,
            pltpu.SemaphoreType.REGULAR,
        ],
        compiler_params=pltpu.CompilerParams(
            collective_id=0, has_side_effects=True, vmem_limit_bytes=60 * 1024 * 1024
        ),
        name="power_attention",
    )(
        jnp.transpose(queries, (1, 0, 2)),
        keys.reshape(rows, hd),
        values.reshape(rows, hd),
        w_out.T,
    )


def solution(mesh):
    body = functools.partial(
        local, parts=mesh.shape["feature"], count=mesh.shape["seq"]
    )
    in_specs = (
        P("seq", "kvhead", None),
        P("seq", "kvhead", None),
        P("seq", "kvhead", None),
        P("kvhead", ("feature", "seq")),
    )
    out_specs = P(("seq", "feature"), "kvhead")
    return jax.shard_map(body, mesh=mesh, in_specs=in_specs, out_specs=out_specs, check_vma=False)
```

```python
import functools

import jax
import jax.numpy as jnp
from jax import lax
from jax.experimental import pallas as pl
from jax.experimental.pallas import tpu as pltpu
from jax.sharding import PartitionSpec as P

MESH = pl.DeviceIdType.MESH
NT = (((1,), (1,)), ((), ()))
F32 = jnp.float32
BF16 = jnp.bfloat16


def halves(x):
    high = x.astype(BF16)
    return high, (x - high.astype(F32)).astype(BF16)


def dot(a, b):
    return jnp.dot(a, b, preferred_element_type=F32)


def dot_nt(a, b):
    return lax.dot_general(a, b, NT, preferred_element_type=F32)


def kernel(
    q_hbm, k_hbm, v_hbm, w_hbm, o_ref,
    qv, kv, wt, qcat, kcat, klow, vcat, rs_src, rs_rcv, den_src, den_rcv, abuf, wh, wl, cpk, c0r, c1r, red, c2r,
    load_sem, kv_send, kv_recv, w_send, w_recv, rs_send, rs_recv, den_send, den_recv, a_send, a_recv,
    c0_send, c0_recv, c1_send, c1_recv, c2_send, c2_recv,
    line_known, side_known, cross_known,
):
    group, rows, hd = q_hbm.shape
    parts = wt.shape[0]
    count = kv.shape[0]
    heads = 2 * parts
    quarter = rows // parts
    half = count // 2
    wide = w_hbm.shape[0]
    rest = wide - hd
    lanes = hd // parts
    f = lax.axis_index("feature")
    k = lax.axis_index("kvhead")
    s = lax.axis_index("seq")
    y, c = lax.div(k, 2), lax.rem(k, 2)
    twin = k + 1 - 2 * c
    seq_half = lax.div(s, half)

    def at_z(d):
        return lax.rem(s + d + count, count)

    def at_x(d):
        return lax.rem(f + d + parts, parts)

    right, left = at_z(1), at_z(-1)

    own = pl.ds(pl.multiple_of(f * quarter, quarter), quarter)
    loads = [
        pltpu.make_async_copy(w_hbm, wt.at[f], load_sem.at[0]),
        pltpu.make_async_copy(k_hbm.at[own], kv.at[s, 0], load_sem.at[1]),
        pltpu.make_async_copy(v_hbm.at[own], kv.at[s, 1], load_sem.at[2]),
        pltpu.make_async_copy(q_hbm, qv, load_sem.at[3]),
    ]
    for load in loads:
        load.start()

    barrier = pltpu.get_barrier_semaphore()

    def signal(semaphore, where):
        pl.semaphore_signal(semaphore, inc=1, device_id=where, device_id_type=MESH)

    beside = [{"kvhead": lax.rem(k + d, heads)} for d in (2, heads - 2)]
    second = [{"seq": at_z(d)} for d in (2, -2)]
    near = [{"feature": at_x(d)} for d in range(1, parts)] + [{"seq": right}, {"seq": left}, {"kvhead": twin}]
    near = near + beside + second
    for where in near:
        signal(barrier, where)
    loads[1].wait()
    loads[2].wait()
    pl.semaphore_wait(barrier, len(near))
    for where in second:
        signal(line_known, where)
    for where in beside:
        signal(side_known, where)

    def known():
        pl.semaphore_wait(line_known, len(second))
        pl.semaphore_wait(side_known, len(beside))
        signal(cross_known, {"kvhead": twin})

    def remote(src, dst, send, recv, where):
        return pltpu.make_async_remote_copy(
            src_ref=src, dst_ref=dst, send_sem=send, recv_sem=recv, device_id=where, device_id_type=MESH
        )

    pieces = 4
    piece = 2 * quarter // pieces
    hops = (2, -2, 1, -1, 3, -3, 4)

    def kv_copy(i, n, slot, where):
        ref = kv.at[slot, n * piece // quarter, pl.ds(n * piece % quarter, piece)]
        return remote(ref, ref, kv_send.at[i, n], kv_recv.at[i, n], {"seq": where})

    def kv_from(i, n):
        return kv_copy(i, n, at_z(-hops[i]), right)

    def kv_out(i, n):
        if i < 4:
            return kv_copy(i, n, s, at_z(hops[i]))
        if i < 6:
            step = 2 if i == 4 else -2
            return kv_copy(i, n, at_z(-step), at_z(step // 2))
        step = 2 if n < pieces // 2 else -2
        return kv_copy(i, n, at_z(-step), at_z(step))

    def kv_take(slot):
        place = pl.ds(pl.multiple_of(slot * quarter, quarter), quarter)
        kh, kl = halves(kv[slot, 0])
        vh, vl = halves(kv[slot, 1])
        kcat[place, :hd] = kh
        kcat[place, hd:] = kh
        klow[place, :] = kl
        vcat[place, :hd] = vh
        vcat[place, hd:] = vl

    for i in range(4):
        for n in range(pieces):
            kv_out(i, n).start()

    def w_copy(i, src, where):
        return remote(src, src, w_send.at[i], w_recv.at[i], {"feature": where})

    w_top, w_low = pl.ds(0, wide // 2), pl.ds(wide // 2, wide // 2)
    w_steps = [
        w_copy(0, wt.at[f], at_x(1)),
        w_copy(1, wt.at[f], at_x(-1)),
        w_copy(2, wt.at[at_x(-1), w_top], at_x(1)),
        w_copy(3, wt.at[at_x(1), w_low], at_x(-1)),
    ]
    w_takes = [
        w_copy(0, wt.at[at_x(-1)], at_x(1)),
        w_copy(1, wt.at[at_x(1)], at_x(-1)),
        w_copy(2, wt.at[at_x(2), w_top], at_x(1)),
        w_copy(3, wt.at[at_x(2), w_low], at_x(-1)),
    ]
    loads[0].wait()
    lead = 1
    early = s < lead

    def w_begin():
        w_steps[0].start()
        w_steps[1].start()

    pl.when(jnp.logical_not(early))(w_begin)

    loads[3].wait()
    for g in range(group):
        qh, ql = halves(qv[g] * (hd ** -0.5))
        qcat[g, :, :hd] = qh
        qcat[g, :, hd:] = ql
    kcat[...] = jnp.zeros_like(kcat)
    klow[...] = jnp.zeros_like(klow)
    vcat[...] = jnp.zeros_like(vcat)
    kv_take(s)
    def kv_second():
        for n in range(pieces):
            kv_from(0, n).wait_recv()
            kv_out(4, n).start()
            if n < pieces // 2:
                kv_out(6, n).start()
            kv_from(1, n).wait_recv()
            kv_out(5, n).start()
            if n >= pieces // 2:
                kv_out(6, n).start()

    @pl.when(s > 0)
    def _():
        kv_second()
        kv_take(at_z(-2))
        kv_take(at_z(2))

    for i in range(2, len(hops)):
        @pl.when(at_z(-hops[i]) < s)
        def _():
            for n in range(pieces):
                kv_from(i, n).wait_recv()
            kv_take(at_z(-hops[i]))


    def rs_copy(d, g):
        to = at_x(d)
        return remote(rs_src.at[g, to], rs_rcv.at[d - 1, g], rs_send.at[d - 1, g], rs_recv.at[d - 1, g], {"feature": to})

    def den_copy(d, g):
        to = at_x(d)
        return remote(
            den_src.at[g, to], den_rcv.at[d - 1, g], den_send.at[d - 1, g], den_recv.at[d - 1, g], {"feature": to}
        )

    shape = (rows, count * quarter)
    column = lax.broadcasted_iota(jnp.int32, shape, 1)
    key_pos = lax.shift_right_logical(column, 6) * rows + f * quarter + jnp.bitwise_and(column, quarter - 1)
    query_pos = s * rows + lax.broadcasted_iota(jnp.int32, shape, 0)
    allowed = key_pos <= query_pos
    diagonal = lax.broadcasted_iota(jnp.int32, (quarter, hd), 0) == lax.broadcasted_iota(jnp.int32, (quarter, hd), 1)

    def head(g, carry):
        scores = dot_nt(qcat[g], kcat[...]) + dot_nt(qcat[g, :, :hd], klow[...])
        squared = jnp.where(allowed, scores * scores, 0.0)
        ph, plow = halves(squared)
        both = dot(ph, vcat[...])
        numerator = both[:, :hd] + both[:, hd:] + dot(plow, vcat[:, :hd])
        denominator = jnp.sum(squared, axis=1, keepdims=True)
        for p in range(parts):
            part = slice(p * quarter, (p + 1) * quarter)
            rs_src[g, p] = numerator[part]
            spread = jnp.where(diagonal, jnp.broadcast_to(denominator[part], (quarter, hd)), 0.0)
            den_src[g, p] = jnp.sum(spread, axis=0, keepdims=True)
        for d in range(1, parts):
            den_copy(d, g).start()
            rs_copy(d, g).start()
        return carry

    lax.fori_loop(0, group, head, 0)

    @pl.when(s == 0)
    def _():
        kv_second()

    pl.when(early)(w_begin)

    def a_copy(i, g, slot, where):
        return remote(abuf.at[slot, g], abuf.at[slot, g], a_send.at[i, g], a_recv.at[slot, g], {"seq": where})

    def a_wait(slot, g):
        a_copy(0, g, slot, right).wait_recv()

    ringed = 3

    def normalize(g):
        for d in range(1, parts):
            den_copy(d, g).wait_recv()
            rs_copy(d, g).wait_recv()
        total = rs_src[g, f] + rs_rcv[0, g]
        line = den_src[g, f] + den_rcv[0, g]
        for d in range(1, parts - 1):
            total = total + rs_rcv[d, g]
            line = line + den_rcv[d, g]
        line = jnp.broadcast_to(line, (quarter, hd))
        denominator = jnp.sum(jnp.where(diagonal, line, 0.0), axis=1, keepdims=True)
        abuf[s, g] = total / (denominator + 1.0)
        if g < ringed:
            @pl.when(early)
            def _():
                for i in range(4):
                    a_out(i, g).start()

            @pl.when(jnp.logical_not(early))
            def _():
                r_out(0, g).start()
                r_out(4, g).start()

        else:
            for i in range(4):
                a_out(i, g).start()

    def r_out(i, g):
        if i == 3:
            step = 2 if g % 2 == 0 else -2
            return a_copy(7 + i, g, at_z(-step), at_z(step))
        if i < 3:
            return a_copy(7 + i, g, at_z(-i), right)
        return a_copy(7 + i, g, at_z(i - 4), left)

    def relay_acts(t, g):
        for slot, i, parity in ((at_z(-t), t, 0), (at_z(t), 4 + t, 1)):
            yield slot, [i, 3] if t == 2 and g % 2 == parity else [i]

    def relay(t, g):
        for slot, acts in relay_acts(t, g):
            @pl.when(slot >= lead)
            def _():
                a_wait(slot, g)
                for i in acts:
                    r_out(i, g).start()

    def a_out(i, g):
        if i < 4:
            return a_copy(i, g, s, at_z(hops[i]))
        if i < 6:
            step = 2 if i == 4 else -2
            return a_copy(i, g, at_z(-step), at_z(step // 2))
        step = 2 if g % 2 == 0 else -2
        return a_copy(i, g, at_z(-step), at_z(step))

    def pass_acts(g):
        for slot, i, parity in ((at_z(-2), 4, 0), (at_z(2), 5, 1)):
            yield slot, [6, i] if g % 2 == parity else [i]

    def pass_on(g, which):
        for slot, acts in pass_acts(g):
            @pl.when(which(slot))
            def _():
                a_wait(slot, g)
                for i in acts:
                    a_out(i, g).start()

    def first(g):
        pass_on(g, lambda slot: slot < lead)

    def forward(g):
        pass_on(g, lambda slot: slot >= lead)

    def arrived(slots):
        for slot in slots:
            away = lax.rem(s - slot + count, count)
            one = (away == 1) | (away == count - 1)
            far = (away > 2) & (away < count - 2)

            @pl.when(far | (one & (slot < lead)))
            def _():
                for g in range(ringed):
                    a_wait(slot, g)

            @pl.when(far | one)
            def _():
                for g in range(ringed, group):
                    a_wait(slot, g)

    def split_weights(p):
        high, low = halves(wt[p])
        main = pl.ds(pl.multiple_of(p * hd, hd), hd)
        tail = pl.ds(pl.multiple_of(parts * hd + p * rest, rest), rest)
        wh[main, :] = high[:hd]
        wl[main, :] = low[:hd]
        wh[tail, :] = high[hd:]
        wl[tail, :] = low[hd:]

    lane_group = lax.div(lax.broadcasted_iota(jnp.int32, (quarter // parts, hd), 1), rest)
    sub = quarter // parts

    def c0_copy(i):
        j = lax.rem(i, half)
        return remote(cpk.at[i], c0r.at[j], c0_send.at[i], c0_recv.at[j], {"kvhead": twin})

    def c1_copy(i, d):
        p = lax.rem(y + d, parts)
        j = lax.rem(i, half)
        return remote(cpk.at[i, p], c1r.at[j, d - 1], c1_send.at[j, d - 1], c1_recv.at[j, d - 1], {"kvhead": 2 * p + c})

    def c2_copy(i):
        j, slot = lax.rem(i, half), lax.rem(s, half)
        return remote(red.at[j], c2r.at[slot], c2_send.at[j], c2_recv.at[slot], {"kvhead": 2 * y + seq_half, "seq": i})

    def mine(i):
        return lax.div(i, half) == c

    def merge(slots):
        for i in slots:
            @pl.when(mine(i))
            def _():
                c0_copy(i).wait_recv()
                for p in range(parts):
                    cpk[i, p] = cpk[i, p] + c0r[lax.rem(i, half), p]
                for d in range(1, parts):
                    c1_copy(i, d).start()

    def finish(slots):
        for i in slots:
            @pl.when(mine(i))
            def _():
                j = lax.rem(i, half)
                total = cpk[i, y]
                for d in range(1, parts):
                    c1_copy(i, d).wait_recv()
                    total = total + c1r[j, d - 1]

                @pl.when(i == s)
                def _():
                    c2r[j] = total

                @pl.when(i != s)
                def _():
                    red[j] = total
                    c2_copy(i).start()

    def project(slots):
        a = jnp.concatenate(
            [jnp.concatenate([abuf[i, g] for g in range(group)], axis=1) for i in slots], axis=0
        )
        n = len(slots) * quarter
        high, low = halves(a)
        both = dot_nt(jnp.concatenate([high, low], axis=0), wh[...])
        out = both[:n] + both[n:] + dot_nt(high, wl[...])
        for m, i in enumerate(slots):
            block = out[m * quarter:(m + 1) * quarter]
            tail = block[:, parts * hd:]
            for p in range(parts):
                cpk[i, p, :quarter] = block[:, p * hd:(p + 1) * hd]
                packed = jnp.zeros((sub, hd), F32)
                for g in range(parts):
                    piece = tail[g * sub:(g + 1) * sub]
                    shift = (rest * (g - p)) % hd
                    if shift:
                        piece = pltpu.roll(piece, shift, 1)
                    packed = jnp.where(lane_group == g, piece, packed)
                cpk[i, p, quarter:] = packed

            @pl.when(jnp.logical_not(mine(i)))
            def _():
                c0_copy(i).start()


    def in_turn(place):
        chosen = jnp.int32(0)
        for here in range(count):
            def away(i):
                steps = min((here - i) % count, (i - here) % count)
                return (0.5, 2.5)[i] if i < 2 and steps > 2 else steps

            chosen = jnp.where(s == here, sorted(range(count), key=away)[place], chosen)
        return chosen

    steps = [[in_turn(n), in_turn(n + 1)] for n in range(0, count, 2)]
    first(0)
    first(1)
    first(2)
    normalize(0)
    first(3)
    normalize(1)
    first(4)
    normalize(2)
    pl.when(early)(lambda: normalize(3))
    pl.when(early)(lambda: normalize(4))
    relay(1, 0)
    pl.when(jnp.logical_not(early))(lambda: normalize(3))
    relay(1, 1)
    pl.when(jnp.logical_not(early))(lambda: normalize(4))
    w_takes[0].wait_recv()
    w_takes[1].wait_recv()
    w_steps[2].start()
    w_steps[3].start()
    for p in (0, -1, 1):
        split_weights(at_x(p))
    relay(1, 2)
    relay(2, 0)
    forward(3)
    relay(2, 1)
    known()
    w_takes[2].wait_recv()
    w_takes[3].wait_recv()
    split_weights(at_x(2))
    forward(4)
    arrived(steps[0])
    project(steps[0])
    pl.when(c == 0)(lambda: merge(steps[0]))
    relay(2, 2)
    arrived(steps[1])
    project(steps[1])
    pl.when(c == 0)(lambda: merge(steps[1]))
    arrived(steps[2])
    project(steps[2])
    pl.when(c == 1)(lambda: merge(steps[0]))
    pl.when(c == 1)(lambda: merge(steps[1]))
    pl.when(c == 0)(lambda: merge(steps[2]))
    arrived(steps[3])
    project(steps[3])
    pl.when(c == 0)(lambda: merge(steps[3]))
    pl.when(c == 1)(lambda: merge(steps[2]))
    pl.when(c == 1)(lambda: merge(steps[3]))
    pl.semaphore_wait(cross_known, 1)
    finish(steps[0])
    finish(steps[1])
    finish(steps[3])
    finish(steps[2])

    for i in range(len(hops)):
        for n in range(pieces):
            kv_out(i, n).wait_send()
    for i in range(2, len(hops)):
        @pl.when(at_z(-hops[i]) > s)
        def _():
            for n in range(pieces):
                kv_from(i, n).wait_recv()

    for copy in w_steps:
        copy.wait_send()

    def drain(g, carry):
        for d in range(1, parts):
            rs_copy(d, g).wait_send()
            den_copy(d, g).wait_send()
        return carry

    lax.fori_loop(0, group, drain, 0)
    for g in range(group):
        if g < ringed:
            @pl.when(early)
            def _():
                for i in range(4):
                    a_out(i, g).wait_send()

            @pl.when(jnp.logical_not(early))
            def _():
                r_out(0, g).wait_send()
                r_out(4, g).wait_send()

            for t in (1, 2):
                for slot, acts in relay_acts(t, g):
                    @pl.when(slot >= lead)
                    def _():
                        for i in acts:
                            r_out(i, g).wait_send()

            for slot, acts in pass_acts(g):
                @pl.when(slot < lead)
                def _():
                    for i in acts:
                        a_out(i, g).wait_send()

        else:
            for i in range(len(hops)):
                a_out(i, g).wait_send()

    def drain_c(i, carry):
        @pl.when(mine(i))
        def _():
            for d in range(1, parts):
                c1_copy(i, d).wait_send()

        @pl.when(jnp.logical_not(mine(i)))
        def _():
            c0_copy(i).wait_send()

        return carry

    lax.fori_loop(0, count, drain_c, 0)

    def arrive(j, carry):
        @pl.when(half * c + j != s)
        def _():
            remote(red.at[j], c2r.at[j], c2_send.at[j], c2_recv.at[j], {"kvhead": twin}).wait_recv()
            c2_copy(half * c + j).wait_send()

        return carry

    lax.fori_loop(0, half, arrive, 0)

    lane = lax.broadcasted_iota(jnp.int32, (quarter, hd), 1)
    for tile in range(parts + 1):
        value = None
        if tile < parts:
            value = c2r[tile, :quarter]
            if tile:
                value = pltpu.roll(value, rest * tile, 1)
        if tile > 0:
            j = tile - 1
            before = c2r[j, :quarter]
            if j:
                before = pltpu.roll(before, rest * j, 1)
            packed = c2r[j, quarter:]
            tail = jnp.concatenate(
                [pltpu.roll(packed, (rest * (j - g)) % hd, 1) if (j - g) % parts else packed for g in range(parts)], axis=0
            )
            value = tail if value is None else jnp.where(lane < rest * tile, tail, value)
            if j:
                value = jnp.where(lane < rest * j, before, value)
        o_ref[:, tile * hd:(tile + 1) * hd] = value


def local(queries, keys, values, w_out, *, parts, count):
    rows, group, hd = queries.shape
    quarter = rows // parts
    depth, wide = w_out.shape
    half = count // 2
    packed = quarter * wide // hd
    columns = parts * wide
    keys_all = count * quarter
    dma = pltpu.SemaphoreType.DMA
    any_space = pl.BlockSpec(memory_space=pl.ANY)
    return pl.pallas_call(
        kernel,
        out_shape=pltpu.VMEM((quarter, half * wide), F32),
        in_specs=[any_space] * 4,
        out_specs=pl.BlockSpec(memory_space=pltpu.VMEM),
        scratch_shapes=[
            pltpu.VMEM((group, rows, hd), F32),
            pltpu.VMEM((count, 2, quarter, hd), F32),
            pltpu.VMEM((parts, wide, depth), F32),
            pltpu.VMEM((group, rows, 2 * hd), BF16),
            pltpu.VMEM((keys_all, 2 * hd), BF16),
            pltpu.VMEM((keys_all, hd), BF16),
            pltpu.VMEM((keys_all, 2 * hd), BF16),
            pltpu.VMEM((group, parts, quarter, hd), F32),
            pltpu.VMEM((parts - 1, group, quarter, hd), F32),
            pltpu.VMEM((group, parts, 1, hd), F32),
            pltpu.VMEM((parts - 1, group, 1, hd), F32),
            pltpu.VMEM((count, group, quarter, hd), F32),
            pltpu.VMEM((columns, depth), BF16),
            pltpu.VMEM((columns, depth), BF16),
            pltpu.VMEM((count, parts, packed, hd), F32),
            pltpu.VMEM((half, parts, packed, hd), F32),
            pltpu.VMEM((half, parts - 1, packed, hd), F32),
            pltpu.VMEM((half, packed, hd), F32),
            pltpu.VMEM((half, packed, hd), F32),
            dma((4,)),
            dma((count - 1, 4)),
            dma((count - 1, 4)),
            dma((4,)),
            dma((4,)),
            dma((parts - 1, group)),
            dma((parts - 1, group)),
            dma((parts - 1, group)),
            dma((parts - 1, group)),
            dma((2 * count - 2, group)),
            dma((count, group)),
            dma((count,)),
            dma((half,)),
            dma((half, parts - 1)),
            dma((half, parts - 1)),
            dma((half,)),
            dma((half,)),
            pltpu.SemaphoreType.REGULAR,
            pltpu.SemaphoreType.REGULAR,
            pltpu.SemaphoreType.REGULAR,
        ],
        compiler_params=pltpu.CompilerParams(
            collective_id=0, has_side_effects=True, vmem_limit_bytes=60 * 1024 * 1024
        ),
        name="power_attention",
    )(
        jnp.transpose(queries, (1, 0, 2)),
        keys.reshape(rows, hd),
        values.reshape(rows, hd),
        w_out.T,
    )


def solution(mesh):
    body = functools.partial(
        local, parts=mesh.shape["feature"], count=mesh.shape["seq"]
    )
    in_specs = (
        P("seq", "kvhead", None),
        P("seq", "kvhead", None),
        P("seq", "kvhead", None),
        P("kvhead", ("feature", "seq")),
    )
    out_specs = P(("seq", "feature"), "kvhead")
    return jax.shard_map(body, mesh=mesh, in_specs=in_specs, out_specs=out_specs, check_vma=False)
```

```python
import functools

import jax
import jax.numpy as jnp
from jax import lax
from jax.experimental import pallas as pl
from jax.experimental.pallas import tpu as pltpu
from jax.sharding import PartitionSpec as P

MESH = pl.DeviceIdType.MESH
NT = (((1,), (1,)), ((), ()))
F32 = jnp.float32
BF16 = jnp.bfloat16


def halves(x):
    high = x.astype(BF16)
    return high, (x - high.astype(F32)).astype(BF16)


def dot(a, b):
    return jnp.dot(a, b, preferred_element_type=F32)


def dot_nt(a, b):
    return lax.dot_general(a, b, NT, preferred_element_type=F32)


def kernel(
    q_hbm, k_hbm, v_hbm, w_hbm, o_ref,
    qv, kv, wt, qcat, kcat, klow, vcat, rs_src, rs_rcv, den_src, den_rcv, abuf, wh, wl, cpk, c0r, c1r, red, c2r,
    load_sem, kv_send, kv_recv, w_send, w_recv, rs_send, rs_recv, den_send, den_recv, a_send, a_recv,
    c0_send, c0_recv, c1_send, c1_recv, c2_send, c2_recv,
    line_known, side_known, cross_known,
):
    group, rows, hd = q_hbm.shape
    parts = wt.shape[0]
    count = kv.shape[0]
    heads = 2 * parts
    quarter = rows // parts
    half = count // 2
    wide = w_hbm.shape[0]
    rest = wide - hd
    lanes = hd // parts
    f = lax.axis_index("feature")
    k = lax.axis_index("kvhead")
    s = lax.axis_index("seq")
    y, c = lax.div(k, 2), lax.rem(k, 2)
    twin = k + 1 - 2 * c
    seq_half = lax.div(s, half)

    def at_z(d):
        return lax.rem(s + d + count, count)

    def at_x(d):
        return lax.rem(f + d + parts, parts)

    right, left = at_z(1), at_z(-1)

    own = pl.ds(pl.multiple_of(f * quarter, quarter), quarter)
    loads = [
        pltpu.make_async_copy(w_hbm, wt.at[f], load_sem.at[0]),
        pltpu.make_async_copy(k_hbm.at[own], kv.at[s, 0], load_sem.at[1]),
        pltpu.make_async_copy(v_hbm.at[own], kv.at[s, 1], load_sem.at[2]),
        pltpu.make_async_copy(q_hbm, qv, load_sem.at[3]),
    ]
    for load in loads:
        load.start()

    barrier = pltpu.get_barrier_semaphore()

    def signal(semaphore, where):
        pl.semaphore_signal(semaphore, inc=1, device_id=where, device_id_type=MESH)

    beside = [{"kvhead": lax.rem(k + d, heads)} for d in (2, heads - 2)]
    second = [{"seq": at_z(d)} for d in (2, -2)]
    near = [{"feature": at_x(d)} for d in range(1, parts)] + [{"seq": right}, {"seq": left}, {"kvhead": twin}]
    near = near + beside + second
    for where in near:
        signal(barrier, where)
    loads[1].wait()
    loads[2].wait()
    pl.semaphore_wait(barrier, len(near))
    for where in second:
        signal(line_known, where)
    for where in beside:
        signal(side_known, where)

    def known():
        pl.semaphore_wait(line_known, len(second))
        pl.semaphore_wait(side_known, len(beside))
        signal(cross_known, {"kvhead": twin})

    def remote(src, dst, send, recv, where):
        return pltpu.make_async_remote_copy(
            src_ref=src, dst_ref=dst, send_sem=send, recv_sem=recv, device_id=where, device_id_type=MESH
        )

    pieces = 4
    piece = 2 * quarter // pieces
    hops = (2, -2, 1, -1, 3, -3, 4)

    def kv_copy(i, n, slot, where):
        ref = kv.at[slot, n * piece // quarter, pl.ds(n * piece % quarter, piece)]
        return remote(ref, ref, kv_send.at[i, n], kv_recv.at[i, n], {"seq": where})

    def kv_from(i, n):
        return kv_copy(i, n, at_z(-hops[i]), right)

    def kv_out(i, n):
        if i < 4:
            return kv_copy(i, n, s, at_z(hops[i]))
        if i < 6:
            step = 2 if i == 4 else -2
            return kv_copy(i, n, at_z(-step), at_z(step // 2))
        step = 2 if n < pieces // 2 else -2
        return kv_copy(i, n, at_z(-step), at_z(step))

    def kv_take(slot):
        place = pl.ds(pl.multiple_of(slot * quarter, quarter), quarter)
        kh, kl = halves(kv[slot, 0])
        vh, vl = halves(kv[slot, 1])
        kcat[place, :hd] = kh
        kcat[place, hd:] = kh
        klow[place, :] = kl
        vcat[place, :hd] = vh
        vcat[place, hd:] = vl

    for i in range(4):
        for n in range(pieces):
            kv_out(i, n).start()

    def w_copy(i, src, where):
        return remote(src, src, w_send.at[i], w_recv.at[i], {"feature": where})

    w_top, w_low = pl.ds(0, wide // 2), pl.ds(wide // 2, wide // 2)
    w_steps = [
        w_copy(0, wt.at[f], at_x(1)),
        w_copy(1, wt.at[f], at_x(-1)),
        w_copy(2, wt.at[at_x(-1), w_top], at_x(1)),
        w_copy(3, wt.at[at_x(1), w_low], at_x(-1)),
    ]
    w_takes = [
        w_copy(0, wt.at[at_x(-1)], at_x(1)),
        w_copy(1, wt.at[at_x(1)], at_x(-1)),
        w_copy(2, wt.at[at_x(2), w_top], at_x(1)),
        w_copy(3, wt.at[at_x(2), w_low], at_x(-1)),
    ]
    loads[0].wait()
    lead = 1
    early = s < lead

    def w_begin():
        w_steps[0].start()
        w_steps[1].start()

    pl.when(jnp.logical_not(early))(w_begin)

    loads[3].wait()
    for g in range(group):
        qh, ql = halves(qv[g] * (hd ** -0.5))
        qcat[g, :, :hd] = qh
        qcat[g, :, hd:] = ql
    kcat[...] = jnp.zeros_like(kcat)
    klow[...] = jnp.zeros_like(klow)
    vcat[...] = jnp.zeros_like(vcat)
    kv_take(s)
    def kv_second():
        for n in range(pieces):
            kv_from(0, n).wait_recv()
            kv_out(4, n).start()
            if n < pieces // 2:
                kv_out(6, n).start()
            kv_from(1, n).wait_recv()
            kv_out(5, n).start()
            if n >= pieces // 2:
                kv_out(6, n).start()

    @pl.when(s > 0)
    def _():
        kv_second()
        kv_take(at_z(-2))
        kv_take(at_z(2))

    for i in range(2, len(hops)):
        @pl.when(at_z(-hops[i]) < s)
        def _():
            for n in range(pieces):
                kv_from(i, n).wait_recv()
            kv_take(at_z(-hops[i]))


    def rs_copy(d, g):
        to = at_x(d)
        return remote(rs_src.at[g, to], rs_rcv.at[d - 1, g], rs_send.at[d - 1, g], rs_recv.at[d - 1, g], {"feature": to})

    def den_copy(d, g):
        to = at_x(d)
        return remote(
            den_src.at[g, to], den_rcv.at[d - 1, g], den_send.at[d - 1, g], den_recv.at[d - 1, g], {"feature": to}
        )

    shape = (rows, count * quarter)
    column = lax.broadcasted_iota(jnp.int32, shape, 1)
    key_pos = lax.shift_right_logical(column, 6) * rows + f * quarter + jnp.bitwise_and(column, quarter - 1)
    query_pos = s * rows + lax.broadcasted_iota(jnp.int32, shape, 0)
    allowed = key_pos <= query_pos
    diagonal = lax.broadcasted_iota(jnp.int32, (quarter, hd), 0) == lax.broadcasted_iota(jnp.int32, (quarter, hd), 1)

    def head(g, carry):
        scores = dot_nt(qcat[g], kcat[...]) + dot_nt(qcat[g, :, :hd], klow[...])
        squared = jnp.where(allowed, scores * scores, 0.0)
        ph, plow = halves(squared)
        both = dot(ph, vcat[...])
        numerator = both[:, :hd] + both[:, hd:] + dot(plow, vcat[:, :hd])
        denominator = jnp.sum(squared, axis=1, keepdims=True)
        for p in range(parts):
            part = slice(p * quarter, (p + 1) * quarter)
            rs_src[g, p] = numerator[part]
            spread = jnp.where(diagonal, jnp.broadcast_to(denominator[part], (quarter, hd)), 0.0)
            den_src[g, p] = jnp.sum(spread, axis=0, keepdims=True)
        for d in range(1, parts):
            den_copy(d, g).start()
            rs_copy(d, g).start()
        return carry

    lax.fori_loop(0, group, head, 0)

    @pl.when(s == 0)
    def _():
        kv_second()

    pl.when(early)(w_begin)

    def a_copy(i, g, slot, where):
        return remote(abuf.at[slot, g], abuf.at[slot, g], a_send.at[i, g], a_recv.at[slot, g], {"seq": where})

    def a_wait(slot, g):
        a_copy(0, g, slot, right).wait_recv()

    ringed = 4

    def normalize(g):
        for d in range(1, parts):
            den_copy(d, g).wait_recv()
            rs_copy(d, g).wait_recv()
        total = rs_src[g, f] + rs_rcv[0, g]
        line = den_src[g, f] + den_rcv[0, g]
        for d in range(1, parts - 1):
            total = total + rs_rcv[d, g]
            line = line + den_rcv[d, g]
        line = jnp.broadcast_to(line, (quarter, hd))
        denominator = jnp.sum(jnp.where(diagonal, line, 0.0), axis=1, keepdims=True)
        abuf[s, g] = total / (denominator + 1.0)
        if g < ringed:
            @pl.when(early)
            def _():
                for i in range(4):
                    a_out(i, g).start()

            @pl.when(jnp.logical_not(early))
            def _():
                r_out(0, g).start()
                r_out(4, g).start()

        else:
            for i in range(4):
                a_out(i, g).start()

    def r_out(i, g):
        if i == 3:
            step = 2 if g % 2 == 0 else -2
            return a_copy(7 + i, g, at_z(-step), at_z(step))
        if i < 3:
            return a_copy(7 + i, g, at_z(-i), right)
        return a_copy(7 + i, g, at_z(i - 4), left)

    def relay_acts(t, g):
        for slot, i, parity in ((at_z(-t), t, 0), (at_z(t), 4 + t, 1)):
            yield slot, [i, 3] if t == 2 and g % 2 == parity else [i]

    def relay(t, g):
        for slot, acts in relay_acts(t, g):
            @pl.when(slot >= lead)
            def _():
                a_wait(slot, g)
                for i in acts:
                    r_out(i, g).start()

    def a_out(i, g):
        if i < 4:
            return a_copy(i, g, s, at_z(hops[i]))
        if i < 6:
            step = 2 if i == 4 else -2
            return a_copy(i, g, at_z(-step), at_z(step // 2))
        step = 2 if g % 2 == 0 else -2
        return a_copy(i, g, at_z(-step), at_z(step))

    def pass_acts(g):
        for slot, i, parity in ((at_z(-2), 4, 0), (at_z(2), 5, 1)):
            yield slot, [6, i] if g % 2 == parity else [i]

    def pass_on(g, which):
        for slot, acts in pass_acts(g):
            @pl.when(which(slot))
            def _():
                a_wait(slot, g)
                for i in acts:
                    a_out(i, g).start()

    def first(g):
        pass_on(g, lambda slot: slot < lead)

    def forward(g):
        pass_on(g, lambda slot: slot >= lead)

    def arrived(slots):
        for slot in slots:
            away = lax.rem(s - slot + count, count)
            one = (away == 1) | (away == count - 1)
            far = (away > 2) & (away < count - 2)

            @pl.when(far | (one & (slot < lead)))
            def _():
                for g in range(ringed):
                    a_wait(slot, g)

            @pl.when(far | one)
            def _():
                for g in range(ringed, group):
                    a_wait(slot, g)

    def split_weights(p):
        high, low = halves(wt[p])
        main = pl.ds(pl.multiple_of(p * hd, hd), hd)
        tail = pl.ds(pl.multiple_of(parts * hd + p * rest, rest), rest)
        wh[main, :] = high[:hd]
        wl[main, :] = low[:hd]
        wh[tail, :] = high[hd:]
        wl[tail, :] = low[hd:]

    lane_group = lax.div(lax.broadcasted_iota(jnp.int32, (quarter // parts, hd), 1), rest)
    sub = quarter // parts

    def c0_copy(i):
        j = lax.rem(i, half)
        return remote(cpk.at[i], c0r.at[j], c0_send.at[i], c0_recv.at[j], {"kvhead": twin})

    def c1_copy(i, d):
        p = lax.rem(y + d, parts)
        j = lax.rem(i, half)
        return remote(cpk.at[i, p], c1r.at[j, d - 1], c1_send.at[j, d - 1], c1_recv.at[j, d - 1], {"kvhead": 2 * p + c})

    def c2_copy(i):
        j, slot = lax.rem(i, half), lax.rem(s, half)
        return remote(red.at[j], c2r.at[slot], c2_send.at[j], c2_recv.at[slot], {"kvhead": 2 * y + seq_half, "seq": i})

    def mine(i):
        return lax.div(i, half) == c

    def merge(slots):
        for i in slots:
            @pl.when(mine(i))
            def _():
                c0_copy(i).wait_recv()
                for p in range(parts):
                    cpk[i, p] = cpk[i, p] + c0r[lax.rem(i, half), p]
                for d in range(1, parts):
                    c1_copy(i, d).start()

    def finish(slots):
        for i in slots:
            @pl.when(mine(i))
            def _():
                j = lax.rem(i, half)
                total = cpk[i, y]
                for d in range(1, parts):
                    c1_copy(i, d).wait_recv()
                    total = total + c1r[j, d - 1]

                @pl.when(i == s)
                def _():
                    c2r[j] = total

                @pl.when(i != s)
                def _():
                    red[j] = total
                    c2_copy(i).start()

    def project(slots):
        a = jnp.concatenate(
            [jnp.concatenate([abuf[i, g] for g in range(group)], axis=1) for i in slots], axis=0
        )
        n = len(slots) * quarter
        high, low = halves(a)
        both = dot_nt(jnp.concatenate([high, low], axis=0), wh[...])
        out = both[:n] + both[n:] + dot_nt(high, wl[...])
        for m, i in enumerate(slots):
            block = out[m * quarter:(m + 1) * quarter]
            tail = block[:, parts * hd:]
            for p in range(parts):
                cpk[i, p, :quarter] = block[:, p * hd:(p + 1) * hd]
                packed = jnp.zeros((sub, hd), F32)
                for g in range(parts):
                    piece = tail[g * sub:(g + 1) * sub]
                    shift = (rest * (g - p)) % hd
                    if shift:
                        piece = pltpu.roll(piece, shift, 1)
                    packed = jnp.where(lane_group == g, piece, packed)
                cpk[i, p, quarter:] = packed

            @pl.when(jnp.logical_not(mine(i)))
            def _():
                c0_copy(i).start()


    def in_turn(place):
        chosen = jnp.int32(0)
        for here in range(count):
            def away(i):
                steps = min((here - i) % count, (i - here) % count)
                return (0.5, 2.5)[i] if i < 2 and steps > 2 else steps

            chosen = jnp.where(s == here, sorted(range(count), key=away)[place], chosen)
        return chosen

    steps = [[in_turn(n), in_turn(n + 1)] for n in range(0, count, 2)]
    first(0)
    first(1)
    first(2)
    normalize(0)
    first(3)
    normalize(1)
    first(4)
    normalize(2)
    pl.when(early)(lambda: normalize(3))
    pl.when(early)(lambda: normalize(4))
    relay(1, 0)
    pl.when(jnp.logical_not(early))(lambda: normalize(3))
    w_takes[0].wait_recv()
    w_takes[1].wait_recv()
    w_steps[2].start()
    w_steps[3].start()
    relay(1, 1)
    pl.when(jnp.logical_not(early))(lambda: normalize(4))
    for p in (0, -1, 1):
        split_weights(at_x(p))
    relay(1, 2)
    relay(2, 0)
    relay(1, 3)
    relay(2, 1)
    known()
    w_takes[2].wait_recv()
    w_takes[3].wait_recv()
    split_weights(at_x(2))
    forward(4)
    relay(2, 2)
    arrived(steps[0])
    project(steps[0])
    pl.when(c == 0)(lambda: merge(steps[0]))
    relay(2, 3)
    arrived(steps[1])
    project(steps[1])
    pl.when(c == 0)(lambda: merge(steps[1]))
    arrived(steps[2])
    project(steps[2])
    pl.when(c == 1)(lambda: merge(steps[0]))
    pl.when(c == 1)(lambda: merge(steps[1]))
    pl.when(c == 0)(lambda: merge(steps[2]))
    arrived(steps[3])
    project(steps[3])
    pl.when(c == 0)(lambda: merge(steps[3]))
    pl.when(c == 1)(lambda: merge(steps[3]))
    pl.when(c == 1)(lambda: merge(steps[2]))
    pl.semaphore_wait(cross_known, 1)
    finish(steps[0])
    finish(steps[1])
    finish(steps[3])
    finish(steps[2])

    for i in range(len(hops)):
        for n in range(pieces):
            kv_out(i, n).wait_send()
    for i in range(2, len(hops)):
        @pl.when(at_z(-hops[i]) > s)
        def _():
            for n in range(pieces):
                kv_from(i, n).wait_recv()

    for copy in w_steps:
        copy.wait_send()

    def drain(g, carry):
        for d in range(1, parts):
            rs_copy(d, g).wait_send()
            den_copy(d, g).wait_send()
        return carry

    lax.fori_loop(0, group, drain, 0)
    for g in range(group):
        if g < ringed:
            @pl.when(early)
            def _():
                for i in range(4):
                    a_out(i, g).wait_send()

            @pl.when(jnp.logical_not(early))
            def _():
                r_out(0, g).wait_send()
                r_out(4, g).wait_send()

            for t in (1, 2):
                for slot, acts in relay_acts(t, g):
                    @pl.when(slot >= lead)
                    def _():
                        for i in acts:
                            r_out(i, g).wait_send()

            for slot, acts in pass_acts(g):
                @pl.when(slot < lead)
                def _():
                    for i in acts:
                        a_out(i, g).wait_send()

        else:
            for i in range(len(hops)):
                a_out(i, g).wait_send()

    def drain_c(i, carry):
        @pl.when(mine(i))
        def _():
            for d in range(1, parts):
                c1_copy(i, d).wait_send()

        @pl.when(jnp.logical_not(mine(i)))
        def _():
            c0_copy(i).wait_send()

        return carry

    lax.fori_loop(0, count, drain_c, 0)

    def arrive(j, carry):
        @pl.when(half * c + j != s)
        def _():
            remote(red.at[j], c2r.at[j], c2_send.at[j], c2_recv.at[j], {"kvhead": twin}).wait_recv()
            c2_copy(half * c + j).wait_send()

        return carry

    lax.fori_loop(0, half, arrive, 0)

    lane = lax.broadcasted_iota(jnp.int32, (quarter, hd), 1)
    for tile in range(parts + 1):
        value = None
        if tile < parts:
            value = c2r[tile, :quarter]
            if tile:
                value = pltpu.roll(value, rest * tile, 1)
        if tile > 0:
            j = tile - 1
            before = c2r[j, :quarter]
            if j:
                before = pltpu.roll(before, rest * j, 1)
            packed = c2r[j, quarter:]
            tail = jnp.concatenate(
                [pltpu.roll(packed, (rest * (j - g)) % hd, 1) if (j - g) % parts else packed for g in range(parts)], axis=0
            )
            value = tail if value is None else jnp.where(lane < rest * tile, tail, value)
            if j:
                value = jnp.where(lane < rest * j, before, value)
        o_ref[:, tile * hd:(tile + 1) * hd] = value


def local(queries, keys, values, w_out, *, parts, count):
    rows, group, hd = queries.shape
    quarter = rows // parts
    depth, wide = w_out.shape
    half = count // 2
    packed = quarter * wide // hd
    columns = parts * wide
    keys_all = count * quarter
    dma = pltpu.SemaphoreType.DMA
    any_space = pl.BlockSpec(memory_space=pl.ANY)
    return pl.pallas_call(
        kernel,
        out_shape=pltpu.VMEM((quarter, half * wide), F32),
        in_specs=[any_space] * 4,
        out_specs=pl.BlockSpec(memory_space=pltpu.VMEM),
        scratch_shapes=[
            pltpu.VMEM((group, rows, hd), F32),
            pltpu.VMEM((count, 2, quarter, hd), F32),
            pltpu.VMEM((parts, wide, depth), F32),
            pltpu.VMEM((group, rows, 2 * hd), BF16),
            pltpu.VMEM((keys_all, 2 * hd), BF16),
            pltpu.VMEM((keys_all, hd), BF16),
            pltpu.VMEM((keys_all, 2 * hd), BF16),
            pltpu.VMEM((group, parts, quarter, hd), F32),
            pltpu.VMEM((parts - 1, group, quarter, hd), F32),
            pltpu.VMEM((group, parts, 1, hd), F32),
            pltpu.VMEM((parts - 1, group, 1, hd), F32),
            pltpu.VMEM((count, group, quarter, hd), F32),
            pltpu.VMEM((columns, depth), BF16),
            pltpu.VMEM((columns, depth), BF16),
            pltpu.VMEM((count, parts, packed, hd), F32),
            pltpu.VMEM((half, parts, packed, hd), F32),
            pltpu.VMEM((half, parts - 1, packed, hd), F32),
            pltpu.VMEM((half, packed, hd), F32),
            pltpu.VMEM((half, packed, hd), F32),
            dma((4,)),
            dma((count - 1, 4)),
            dma((count - 1, 4)),
            dma((4,)),
            dma((4,)),
            dma((parts - 1, group)),
            dma((parts - 1, group)),
            dma((parts - 1, group)),
            dma((parts - 1, group)),
            dma((2 * count - 2, group)),
            dma((count, group)),
            dma((count,)),
            dma((half,)),
            dma((half, parts - 1)),
            dma((half, parts - 1)),
            dma((half,)),
            dma((half,)),
            pltpu.SemaphoreType.REGULAR,
            pltpu.SemaphoreType.REGULAR,
            pltpu.SemaphoreType.REGULAR,
        ],
        compiler_params=pltpu.CompilerParams(
            collective_id=0, has_side_effects=True, vmem_limit_bytes=60 * 1024 * 1024
        ),
        name="power_attention",
    )(
        jnp.transpose(queries, (1, 0, 2)),
        keys.reshape(rows, hd),
        values.reshape(rows, hd),
        w_out.T,
    )


def solution(mesh):
    body = functools.partial(
        local, parts=mesh.shape["feature"], count=mesh.shape["seq"]
    )
    in_specs = (
        P("seq", "kvhead", None),
        P("seq", "kvhead", None),
        P("seq", "kvhead", None),
        P("kvhead", ("feature", "seq")),
    )
    out_specs = P(("seq", "feature"), "kvhead")
    return jax.shard_map(body, mesh=mesh, in_specs=in_specs, out_specs=out_specs, check_vma=False)
```

```python
import functools

import jax
import jax.numpy as jnp
from jax import lax
from jax.experimental import pallas as pl
from jax.experimental.pallas import tpu as pltpu
from jax.sharding import PartitionSpec as P

MESH = pl.DeviceIdType.MESH
NT = (((1,), (1,)), ((), ()))
F32 = jnp.float32
BF16 = jnp.bfloat16


def halves(x):
    high = x.astype(BF16)
    return high, (x - high.astype(F32)).astype(BF16)


def dot(a, b):
    return jnp.dot(a, b, preferred_element_type=F32)


def dot_nt(a, b):
    return lax.dot_general(a, b, NT, preferred_element_type=F32)


def kernel(
    q_hbm, k_hbm, v_hbm, w_hbm, o_ref,
    qv, kv, wt, qcat, kcat, klow, vcat, rs_src, rs_rcv, den_src, den_rcv, abuf, wh, wl, cpk, c0r, c1r, red, c2r,
    load_sem, kv_send, kv_recv, w_send, w_recv, rs_send, rs_recv, den_send, den_recv, a_send, a_recv,
    c0_send, c0_recv, c1_send, c1_recv, c2_send, c2_recv,
    line_known, side_known, cross_known,
):
    group, rows, hd = q_hbm.shape
    parts = wt.shape[0]
    count = kv.shape[0]
    heads = 2 * parts
    quarter = rows // parts
    half = count // 2
    wide = w_hbm.shape[0]
    rest = wide - hd
    lanes = hd // parts
    f = lax.axis_index("feature")
    k = lax.axis_index("kvhead")
    s = lax.axis_index("seq")
    y, c = lax.div(k, 2), lax.rem(k, 2)
    twin = k + 1 - 2 * c
    seq_half = lax.div(s, half)

    def at_z(d):
        return lax.rem(s + d + count, count)

    def at_x(d):
        return lax.rem(f + d + parts, parts)

    right, left = at_z(1), at_z(-1)

    own = pl.ds(pl.multiple_of(f * quarter, quarter), quarter)
    loads = [
        pltpu.make_async_copy(w_hbm, wt.at[f], load_sem.at[0]),
        pltpu.make_async_copy(k_hbm.at[own], kv.at[s, 0], load_sem.at[1]),
        pltpu.make_async_copy(v_hbm.at[own], kv.at[s, 1], load_sem.at[2]),
        pltpu.make_async_copy(q_hbm, qv, load_sem.at[3]),
    ]
    for load in loads:
        load.start()

    barrier = pltpu.get_barrier_semaphore()

    def signal(semaphore, where):
        pl.semaphore_signal(semaphore, inc=1, device_id=where, device_id_type=MESH)

    beside = [{"kvhead": lax.rem(k + d, heads)} for d in (2, heads - 2)]
    second = [{"seq": at_z(d)} for d in (2, -2)]
    near = [{"feature": at_x(d)} for d in range(1, parts)] + [{"seq": right}, {"seq": left}, {"kvhead": twin}]
    near = near + beside + second
    for where in near:
        signal(barrier, where)
    loads[1].wait()
    loads[2].wait()
    pl.semaphore_wait(barrier, len(near))
    for where in second:
        signal(line_known, where)
    for where in beside:
        signal(side_known, where)

    def known():
        pl.semaphore_wait(line_known, len(second))
        pl.semaphore_wait(side_known, len(beside))
        signal(cross_known, {"kvhead": twin})

    def remote(src, dst, send, recv, where):
        return pltpu.make_async_remote_copy(
            src_ref=src, dst_ref=dst, send_sem=send, recv_sem=recv, device_id=where, device_id_type=MESH
        )

    pieces = 4
    piece = 2 * quarter // pieces
    hops = (2, -2, 1, -1, 3, -3, 4)

    def kv_copy(i, n, slot, where):
        ref = kv.at[slot, n * piece // quarter, pl.ds(n * piece % quarter, piece)]
        return remote(ref, ref, kv_send.at[i, n], kv_recv.at[i, n], {"seq": where})

    def kv_from(i, n):
        return kv_copy(i, n, at_z(-hops[i]), right)

    def kv_out(i, n):
        if i < 4:
            return kv_copy(i, n, s, at_z(hops[i]))
        if i < 6:
            step = 2 if i == 4 else -2
            return kv_copy(i, n, at_z(-step), at_z(step // 2))
        step = 2 if n < pieces // 2 else -2
        return kv_copy(i, n, at_z(-step), at_z(step))

    def kv_take(slot):
        place = pl.ds(pl.multiple_of(slot * quarter, quarter), quarter)
        kh, kl = halves(kv[slot, 0])
        vh, vl = halves(kv[slot, 1])
        kcat[place, :hd] = kh
        kcat[place, hd:] = kh
        klow[place, :] = kl
        vcat[place, :hd] = vh
        vcat[place, hd:] = vl

    for i in range(4):
        for n in range(pieces):
            kv_out(i, n).start()

    def w_copy(i, src, where):
        return remote(src, src, w_send.at[i], w_recv.at[i], {"feature": where})

    w_top, w_low = pl.ds(0, wide // 2), pl.ds(wide // 2, wide // 2)
    w_steps = [
        w_copy(0, wt.at[f], at_x(1)),
        w_copy(1, wt.at[f], at_x(-1)),
        w_copy(2, wt.at[at_x(-1), w_top], at_x(1)),
        w_copy(3, wt.at[at_x(1), w_low], at_x(-1)),
    ]
    w_takes = [
        w_copy(0, wt.at[at_x(-1)], at_x(1)),
        w_copy(1, wt.at[at_x(1)], at_x(-1)),
        w_copy(2, wt.at[at_x(2), w_top], at_x(1)),
        w_copy(3, wt.at[at_x(2), w_low], at_x(-1)),
    ]
    loads[0].wait()
    lead = 1
    early = s < lead

    def w_begin():
        w_steps[0].start()
        w_steps[1].start()

    pl.when(jnp.logical_not(early))(w_begin)

    loads[3].wait()
    for g in range(group):
        qh, ql = halves(qv[g] * (hd ** -0.5))
        qcat[g, :, :hd] = qh
        qcat[g, :, hd:] = ql
    kcat[...] = jnp.zeros_like(kcat)
    klow[...] = jnp.zeros_like(klow)
    vcat[...] = jnp.zeros_like(vcat)
    kv_take(s)
    def kv_second():
        for n in range(pieces):
            kv_from(0, n).wait_recv()
            kv_out(4, n).start()
            if n < pieces // 2:
                kv_out(6, n).start()
            kv_from(1, n).wait_recv()
            kv_out(5, n).start()
            if n >= pieces // 2:
                kv_out(6, n).start()

    @pl.when(s > 0)
    def _():
        kv_second()
        kv_take(at_z(-2))
        kv_take(at_z(2))

    for i in range(2, len(hops)):
        @pl.when(at_z(-hops[i]) < s)
        def _():
            for n in range(pieces):
                kv_from(i, n).wait_recv()
            kv_take(at_z(-hops[i]))


    def rs_copy(d, g):
        to = at_x(d)
        return remote(rs_src.at[g, to], rs_rcv.at[d - 1, g], rs_send.at[d - 1, g], rs_recv.at[d - 1, g], {"feature": to})

    def den_copy(d, g):
        to = at_x(d)
        return remote(
            den_src.at[g, to], den_rcv.at[d - 1, g], den_send.at[d - 1, g], den_recv.at[d - 1, g], {"feature": to}
        )

    shape = (rows, count * quarter)
    column = lax.broadcasted_iota(jnp.int32, shape, 1)
    key_pos = lax.shift_right_logical(column, 6) * rows + f * quarter + jnp.bitwise_and(column, quarter - 1)
    query_pos = s * rows + lax.broadcasted_iota(jnp.int32, shape, 0)
    allowed = key_pos <= query_pos
    diagonal = lax.broadcasted_iota(jnp.int32, (quarter, hd), 0) == lax.broadcasted_iota(jnp.int32, (quarter, hd), 1)

    def head(g, carry):
        scores = dot_nt(qcat[g], kcat[...]) + dot_nt(qcat[g, :, :hd], klow[...])
        squared = jnp.where(allowed, scores * scores, 0.0)
        ph, plow = halves(squared)
        both = dot(ph, vcat[...])
        numerator = both[:, :hd] + both[:, hd:] + dot(plow, vcat[:, :hd])
        denominator = jnp.sum(squared, axis=1, keepdims=True)
        for p in range(parts):
            part = slice(p * quarter, (p + 1) * quarter)
            rs_src[g, p] = numerator[part]
            spread = jnp.where(diagonal, jnp.broadcast_to(denominator[part], (quarter, hd)), 0.0)
            den_src[g, p] = jnp.sum(spread, axis=0, keepdims=True)
        for d in (2, 1, 3):
            den_copy(d, g).start()
            rs_copy(d, g).start()
        return carry

    lax.fori_loop(0, group, head, 0)

    @pl.when(s == 0)
    def _():
        kv_second()

    pl.when(early)(w_begin)

    def a_copy(i, g, slot, where):
        return remote(abuf.at[slot, g], abuf.at[slot, g], a_send.at[i, g], a_recv.at[slot, g], {"seq": where})

    def a_wait(slot, g):
        a_copy(0, g, slot, right).wait_recv()

    ringed = 3

    def normalize(g):
        for d in range(1, parts):
            den_copy(d, g).wait_recv()
            rs_copy(d, g).wait_recv()
        total = rs_src[g, f] + rs_rcv[0, g]
        line = den_src[g, f] + den_rcv[0, g]
        for d in range(1, parts - 1):
            total = total + rs_rcv[d, g]
            line = line + den_rcv[d, g]
        line = jnp.broadcast_to(line, (quarter, hd))
        denominator = jnp.sum(jnp.where(diagonal, line, 0.0), axis=1, keepdims=True)
        abuf[s, g] = total / (denominator + 1.0)
        if g < ringed:
            @pl.when(early)
            def _():
                for i in range(4):
                    a_out(i, g).start()

            @pl.when(jnp.logical_not(early))
            def _():
                r_out(0, g).start()
                r_out(4, g).start()

        else:
            for i in range(4):
                a_out(i, g).start()

    def r_out(i, g):
        if i == 3:
            step = 2 if g % 2 == 0 else -2
            return a_copy(7 + i, g, at_z(-step), at_z(step))
        if i < 3:
            return a_copy(7 + i, g, at_z(-i), right)
        return a_copy(7 + i, g, at_z(i - 4), left)

    def relay_acts(t, g):
        for slot, i, parity in ((at_z(-t), t, 0), (at_z(t), 4 + t, 1)):
            yield slot, [i, 3] if t == 2 and g % 2 == parity else [i]

    def relay(t, g):
        for slot, acts in relay_acts(t, g):
            @pl.when(slot >= lead)
            def _():
                a_wait(slot, g)
                for i in acts:
                    r_out(i, g).start()

    def a_out(i, g):
        if i < 4:
            return a_copy(i, g, s, at_z(hops[i]))
        if i < 6:
            step = 2 if i == 4 else -2
            return a_copy(i, g, at_z(-step), at_z(step // 2))
        step = 2 if g % 2 == 0 else -2
        return a_copy(i, g, at_z(-step), at_z(step))

    def pass_acts(g):
        for slot, i, parity in ((at_z(-2), 4, 0), (at_z(2), 5, 1)):
            yield slot, [6, i] if g % 2 == parity else [i]

    def pass_on(g, which):
        for slot, acts in pass_acts(g):
            @pl.when(which(slot))
            def _():
                a_wait(slot, g)
                for i in acts:
                    a_out(i, g).start()

    def first(g):
        pass_on(g, lambda slot: slot < lead)

    def forward(g):
        pass_on(g, lambda slot: slot >= lead)

    def arrived(slots):
        for slot in slots:
            away = lax.rem(s - slot + count, count)
            one = (away == 1) | (away == count - 1)
            far = (away > 2) & (away < count - 2)

            @pl.when(far | (one & (slot < lead)))
            def _():
                for g in range(ringed):
                    a_wait(slot, g)

            @pl.when(far | one)
            def _():
                for g in range(ringed, group):
                    a_wait(slot, g)

    def split_weights(p):
        high, low = halves(wt[p])
        main = pl.ds(pl.multiple_of(p * hd, hd), hd)
        tail = pl.ds(pl.multiple_of(parts * hd + p * rest, rest), rest)
        wh[main, :] = high[:hd]
        wl[main, :] = low[:hd]
        wh[tail, :] = high[hd:]
        wl[tail, :] = low[hd:]

    lane_group = lax.div(lax.broadcasted_iota(jnp.int32, (quarter // parts, hd), 1), rest)
    sub = quarter // parts

    def c0_copy(i):
        j = lax.rem(i, half)
        return remote(cpk.at[i], c0r.at[j], c0_send.at[i], c0_recv.at[j], {"kvhead": twin})

    def c1_copy(i, d):
        p = lax.rem(y + d, parts)
        j = lax.rem(i, half)
        return remote(cpk.at[i, p], c1r.at[j, d - 1], c1_send.at[j, d - 1], c1_recv.at[j, d - 1], {"kvhead": 2 * p + c})

    def c2_copy(i):
        j, slot = lax.rem(i, half), lax.rem(s, half)
        return remote(red.at[j], c2r.at[slot], c2_send.at[j], c2_recv.at[slot], {"kvhead": 2 * y + seq_half, "seq": i})

    def mine(i):
        return lax.div(i, half) == c

    def merge(slots):
        for i in slots:
            @pl.when(mine(i))
            def _():
                c0_copy(i).wait_recv()
                for p in range(parts):
                    cpk[i, p] = cpk[i, p] + c0r[lax.rem(i, half), p]
                for d in (2, 1, 3):
                    c1_copy(i, d).start()

    def finish(slots):
        for i in slots:
            @pl.when(mine(i))
            def _():
                j = lax.rem(i, half)
                total = cpk[i, y]
                for d in range(1, parts):
                    c1_copy(i, d).wait_recv()
                    total = total + c1r[j, d - 1]

                @pl.when(i == s)
                def _():
                    c2r[j] = total

                @pl.when(i != s)
                def _():
                    red[j] = total
                    c2_copy(i).start()

    def project(slots):
        a = jnp.concatenate(
            [jnp.concatenate([abuf[i, g] for g in range(group)], axis=1) for i in slots], axis=0
        )
        n = len(slots) * quarter
        high, low = halves(a)
        both = dot_nt(jnp.concatenate([high, low], axis=0), wh[...])
        out = both[:n] + both[n:] + dot_nt(high, wl[...])
        for m, i in enumerate(slots):
            block = out[m * quarter:(m + 1) * quarter]
            tail = block[:, parts * hd:]
            for p in range(parts):
                cpk[i, p, :quarter] = block[:, p * hd:(p + 1) * hd]
                packed = jnp.zeros((sub, hd), F32)
                for g in range(parts):
                    piece = tail[g * sub:(g + 1) * sub]
                    shift = (rest * (g - p)) % hd
                    if shift:
                        piece = pltpu.roll(piece, shift, 1)
                    packed = jnp.where(lane_group == g, piece, packed)
                cpk[i, p, quarter:] = packed

            @pl.when(jnp.logical_not(mine(i)))
            def _():
                c0_copy(i).start()


    def in_turn(place):
        chosen = jnp.int32(0)
        for here in range(count):
            def away(i):
                steps = min((here - i) % count, (i - here) % count)
                return (0.5, 2.5)[i] if i < 2 and steps > 2 else steps

            chosen = jnp.where(s == here, sorted(range(count), key=away)[place], chosen)
        return chosen

    steps = [[in_turn(n), in_turn(n + 1)] for n in range(0, count, 2)]
    first(0)
    first(1)
    first(2)
    normalize(0)
    first(3)
    normalize(1)
    first(4)
    normalize(2)
    pl.when(early)(lambda: normalize(3))
    pl.when(early)(lambda: normalize(4))
    relay(1, 0)
    pl.when(jnp.logical_not(early))(lambda: normalize(3))
    relay(1, 1)
    pl.when(jnp.logical_not(early))(lambda: normalize(4))
    w_takes[0].wait_recv()
    w_takes[1].wait_recv()
    w_steps[2].start()
    w_steps[3].start()
    for p in (0, -1, 1):
        split_weights(at_x(p))
    relay(1, 2)
    relay(2, 0)
    forward(3)
    relay(2, 1)
    known()
    w_takes[2].wait_recv()
    w_takes[3].wait_recv()
    split_weights(at_x(2))
    forward(4)
    arrived(steps[0])
    project(steps[0])
    pl.when(c == 0)(lambda: merge(steps[0]))
    relay(2, 2)
    arrived(steps[1])
    project(steps[1])
    pl.when(c == 0)(lambda: merge(steps[1]))
    arrived(steps[2])
    project(steps[2])
    pl.when(c == 1)(lambda: merge(steps[0]))
    pl.when(c == 1)(lambda: merge(steps[1]))
    pl.when(c == 0)(lambda: merge(steps[2]))
    arrived(steps[3])
    project(steps[3])
    pl.when(c == 0)(lambda: merge(steps[3]))
    pl.when(c == 1)(lambda: merge(steps[2]))
    pl.when(c == 1)(lambda: merge(steps[3]))
    pl.semaphore_wait(cross_known, 1)
    finish(steps[0])
    finish(steps[1])
    finish(steps[3])
    finish(steps[2])

    for i in range(len(hops)):
        for n in range(pieces):
            kv_out(i, n).wait_send()
    for i in range(2, len(hops)):
        @pl.when(at_z(-hops[i]) > s)
        def _():
            for n in range(pieces):
                kv_from(i, n).wait_recv()

    for copy in w_steps:
        copy.wait_send()

    def drain(g, carry):
        for d in range(1, parts):
            rs_copy(d, g).wait_send()
            den_copy(d, g).wait_send()
        return carry

    lax.fori_loop(0, group, drain, 0)
    for g in range(group):
        if g < ringed:
            @pl.when(early)
            def _():
                for i in range(4):
                    a_out(i, g).wait_send()

            @pl.when(jnp.logical_not(early))
            def _():
                r_out(0, g).wait_send()
                r_out(4, g).wait_send()

            for t in (1, 2):
                for slot, acts in relay_acts(t, g):
                    @pl.when(slot >= lead)
                    def _():
                        for i in acts:
                            r_out(i, g).wait_send()

            for slot, acts in pass_acts(g):
                @pl.when(slot < lead)
                def _():
                    for i in acts:
                        a_out(i, g).wait_send()

        else:
            for i in range(len(hops)):
                a_out(i, g).wait_send()

    def drain_c(i, carry):
        @pl.when(mine(i))
        def _():
            for d in range(1, parts):
                c1_copy(i, d).wait_send()

        @pl.when(jnp.logical_not(mine(i)))
        def _():
            c0_copy(i).wait_send()

        return carry

    lax.fori_loop(0, count, drain_c, 0)

    def arrive(j, carry):
        @pl.when(half * c + j != s)
        def _():
            remote(red.at[j], c2r.at[j], c2_send.at[j], c2_recv.at[j], {"kvhead": twin}).wait_recv()
            c2_copy(half * c + j).wait_send()

        return carry

    lax.fori_loop(0, half, arrive, 0)

    lane = lax.broadcasted_iota(jnp.int32, (quarter, hd), 1)
    for tile in range(parts + 1):
        value = None
        if tile < parts:
            value = c2r[tile, :quarter]
            if tile:
                value = pltpu.roll(value, rest * tile, 1)
        if tile > 0:
            j = tile - 1
            before = c2r[j, :quarter]
            if j:
                before = pltpu.roll(before, rest * j, 1)
            packed = c2r[j, quarter:]
            tail = jnp.concatenate(
                [pltpu.roll(packed, (rest * (j - g)) % hd, 1) if (j - g) % parts else packed for g in range(parts)], axis=0
            )
            value = tail if value is None else jnp.where(lane < rest * tile, tail, value)
            if j:
                value = jnp.where(lane < rest * j, before, value)
        o_ref[:, tile * hd:(tile + 1) * hd] = value


def local(queries, keys, values, w_out, *, parts, count):
    rows, group, hd = queries.shape
    quarter = rows // parts
    depth, wide = w_out.shape
    half = count // 2
    packed = quarter * wide // hd
    columns = parts * wide
    keys_all = count * quarter
    dma = pltpu.SemaphoreType.DMA
    any_space = pl.BlockSpec(memory_space=pl.ANY)
    return pl.pallas_call(
        kernel,
        out_shape=pltpu.VMEM((quarter, half * wide), F32),
        in_specs=[any_space] * 4,
        out_specs=pl.BlockSpec(memory_space=pltpu.VMEM),
        scratch_shapes=[
            pltpu.VMEM((group, rows, hd), F32),
            pltpu.VMEM((count, 2, quarter, hd), F32),
            pltpu.VMEM((parts, wide, depth), F32),
            pltpu.VMEM((group, rows, 2 * hd), BF16),
            pltpu.VMEM((keys_all, 2 * hd), BF16),
            pltpu.VMEM((keys_all, hd), BF16),
            pltpu.VMEM((keys_all, 2 * hd), BF16),
            pltpu.VMEM((group, parts, quarter, hd), F32),
            pltpu.VMEM((parts - 1, group, quarter, hd), F32),
            pltpu.VMEM((group, parts, 1, hd), F32),
            pltpu.VMEM((parts - 1, group, 1, hd), F32),
            pltpu.VMEM((count, group, quarter, hd), F32),
            pltpu.VMEM((columns, depth), BF16),
            pltpu.VMEM((columns, depth), BF16),
            pltpu.VMEM((count, parts, packed, hd), F32),
            pltpu.VMEM((half, parts, packed, hd), F32),
            pltpu.VMEM((half, parts - 1, packed, hd), F32),
            pltpu.VMEM((half, packed, hd), F32),
            pltpu.VMEM((half, packed, hd), F32),
            dma((4,)),
            dma((count - 1, 4)),
            dma((count - 1, 4)),
            dma((4,)),
            dma((4,)),
            dma((parts - 1, group)),
            dma((parts - 1, group)),
            dma((parts - 1, group)),
            dma((parts - 1, group)),
            dma((2 * count - 2, group)),
            dma((count, group)),
            dma((count,)),
            dma((half,)),
            dma((half, parts - 1)),
            dma((half, parts - 1)),
            dma((half,)),
            dma((half,)),
            pltpu.SemaphoreType.REGULAR,
            pltpu.SemaphoreType.REGULAR,
            pltpu.SemaphoreType.REGULAR,
        ],
        compiler_params=pltpu.CompilerParams(
            collective_id=0, has_side_effects=True, vmem_limit_bytes=60 * 1024 * 1024
        ),
        name="power_attention",
    )(
        jnp.transpose(queries, (1, 0, 2)),
        keys.reshape(rows, hd),
        values.reshape(rows, hd),
        w_out.T,
    )


def solution(mesh):
    body = functools.partial(
        local, parts=mesh.shape["feature"], count=mesh.shape["seq"]
    )
    in_specs = (
        P("seq", "kvhead", None),
        P("seq", "kvhead", None),
        P("seq", "kvhead", None),
        P("kvhead", ("feature", "seq")),
    )
    out_specs = P(("seq", "feature"), "kvhead")
    return jax.shard_map(body, mesh=mesh, in_specs=in_specs, out_specs=out_specs, check_vma=False)
```
